32 devices in a mesh: fsdp: 8 (over y, x, core), tp: 4 (over z).
Axes of the slice: x: 2, y: 2, z: 4, core: 2. Of those that a mesh axis runs over, the one named last changes fastest.
Arguments:
- activations: bfloat16 [4096, 5120], P('fsdp'), may hold values from -80 to 80
- cotangent: bfloat16 [4096, 5120], P('fsdp'), may hold values from -80 to 80
- lengths: int32 [16], P('fsdp'), may hold values from 64 to 256, as said below
- grow_operator: bfloat16 [5120, 4096], P('fsdp', 'tp'), may hold values from -0.078125 to 0.078125
- proxy_weight: bfloat16 [4096, 4096], P('fsdp', 'tp'), may hold values from -0.09375 to 0.09375
Outputs:
- update: bfloat16 [5120, 4096], P('fsdp', 'tp')
The draws below stay inside these ranges and needn't reach their ends.
Inputs may be any that keep to these rules, and one draw needn't show every extreme that they name: `lengths`: each entry is the length of one sequence; at least one is 256 and at least one is 64.
All inputs are finite; a program needn't handle non-finite values.
Results may differ from the reference program's by a relative error of at most 0.0057.
Values may be sent and summed in bfloat16 or wider, within the bound.
No kernel may reach another device: no remote copies, remote signals or barrier semaphores. Data moves between devices by JAX's collectives and lax.ppermute only.
A program may use at most 128 MiB of HBM per device.

```python
import jax
import jax.numpy as jnp
from jax import lax

D = 5120
PD = 4096
LEN = 256
SEQS = 2
TOKENS = 4096
N_FSDP = 8


def column_scale(key, width):
    ramp = jnp.arange(width, dtype=jnp.float32) / width
    rough = jax.random.uniform(key, (width,), jnp.float32)
    return 10.0 ** (0.5 * ramp + 0.5 * rough)


def scaled_rows(key, rows_total, width):
    keys = jax.random.split(key, 2)
    scale = column_scale(keys[0], width)
    values = jnp.clip(jax.random.normal(keys[1], (rows_total, width), jnp.float32), -4.0, 4.0)
    return jnp.clip(values * scale[None, :], -80.0, 80.0)


def draw_activations(key, part):
    return scaled_rows(jax.random.fold_in(key, 11), TOKENS, D).astype(jnp.bfloat16)


def draw_cotangent(key, part):
    return scaled_rows(jax.random.fold_in(key, 23), TOKENS, D).astype(jnp.bfloat16)


def draw_lengths(key, part):
    drawn = jax.random.randint(jax.random.fold_in(key, 37), (SEQS * N_FSDP,), LEN // 4, LEN + 1, dtype=jnp.int32)
    return drawn.at[0].set(LEN).at[1].set(LEN // 4)


def shard_levels(rng, extent, pieces, least, top_value):
    def one(position, shards_of):
        heights = jax.random.uniform(jax.random.fold_in(jax.random.fold_in(rng, 6), position), (shards_of,), jnp.float32, least / len(pieces), top_value / len(pieces))
        return jnp.repeat(jnp.exp(heights), extent[position] // shards_of).reshape((-1,) + (1,) * (len(extent) - position - 1))

    gain = one(*pieces[0])
    for cut in pieces[1:]:
        gain = gain * one(*cut)
    return gain


def bell_draw(own_key, shape, scale, most, cuts=(), kind=jnp.bfloat16):
    values = jax.random.normal(own_key, shape, jnp.float32) * scale
    if len(cuts) > 0:
        values = shard_levels(own_key, shape, cuts, -0.22, 0.18) * values
    return jnp.clip(values, min=-most, max=most).astype(kind)


def setup_inputs(seed: int = 0) -> dict:
    splits = jax.random.split(jax.random.key(seed), 6)
    activations = draw_activations(jax.random.fold_in(splits[5], 71), 0)
    cotangent = draw_cotangent(jax.random.fold_in(splits[5], 71), 0)
    lengths = draw_lengths(jax.random.fold_in(splits[5], 71), 0)
    grow_operator = bell_draw(splits[3], (D, PD), D ** -0.5, 0.078125, ((0, 8), (1, 4)))
    proxy_weight = bell_draw(splits[4], (PD, PD), PD ** -0.5, 0.09375, ((0, 8), (1, 4)))
    return {"activations": activations, "cotangent": cotangent, "lengths": lengths, "grow_operator": grow_operator, "proxy_weight": proxy_weight}


def contract_tokens(left, right):
    return lax.dot_general(left, right, (((0,), (0,)), ((), ())), preferred_element_type=jnp.float32)

def contract_last(left, right):
    return lax.dot_general(left, right, (((1,), (1,)), ((), ())), preferred_element_type=jnp.float32)

def reference(activations, cotangent, lengths, grow_operator, proxy_weight):
    keep_mask = (jnp.arange(LEN, dtype=jnp.int32)[None, :] < lengths[:, None]).reshape(-1)
    grad_rows = jnp.where(keep_mask[:, None], cotangent, jnp.zeros_like(cotangent))
    forward = jnp.dot(activations, grow_operator, preferred_element_type=jnp.float32).astype(jnp.bfloat16)
    proxy_out = contract_last(forward, proxy_weight).astype(jnp.bfloat16)
    back = jnp.dot(grad_rows, grow_operator, preferred_element_type=jnp.float32).astype(jnp.bfloat16)
    delta = jnp.dot(back, proxy_weight, preferred_element_type=jnp.float32).astype(jnp.bfloat16)
    grad = contract_tokens(activations, delta) + contract_tokens(grad_rows, proxy_out)
    mean_sq = jnp.mean(grad * grad)
    return (grad * lax.rsqrt(mean_sq + 1e-06)).astype(jnp.bfloat16)
```

```python
import jax
import jax.numpy as jnp
from jax import lax
from jax.sharding import PartitionSpec as P


LEN = 256
CHUNKS = 2
BF = jnp.bfloat16
F32 = jnp.float32


def dot(left, right, dims):
    return lax.dot_general(left, right, ((dims[:1], dims[1:]), ((), ())), preferred_element_type=F32)


def flip(value, axis, size, bit):
    return lax.ppermute(value, axis, [(i, i ^ bit) for i in range(size)])


def after(value, *others):
    return lax.optimization_barrier((value,) + others)[0]


def masks_of(bits):
    masks = [0]
    for bit in bits:
        masks = masks + [m | bit for m in masks]
    return sorted(masks, key=lambda m: (bin(m).count("1"), m))


def gather_blocks(shard, size, bits):
    got = {0: shard}
    half = shard.shape[0] // 2
    for mask in masks_of(bits)[1:]:
        inside = [bit for bit in bits if mask & bit]
        if len(inside) == 1:
            got[mask] = flip(shard, "fsdp", size, inside[0])
        else:
            first, last = inside[0], inside[-1]
            low = flip(got[mask ^ last][:half], "fsdp", size, last)
            high = flip(got[mask ^ first][half:], "fsdp", size, first)
            got[mask] = jnp.concatenate([low, high], axis=0)
    for mask in masks_of(bits):
        got[mask ^ 1] = flip(got[mask], "fsdp", size, 1)
    return got


def per_device(n_fsdp, n_tp, activations, cotangent, lengths, grow_operator, proxy_weight):
    me = lax.axis_index("fsdp")
    at = lax.axis_index("tp")
    bits = []
    while 2 << len(bits) < n_fsdp:
        bits.append(2 << len(bits))
    keeps = masks_of(bits)
    order = keeps + [m ^ 1 for m in keeps]
    tokens = activations.shape[0]
    rows, width = grow_operator.shape
    depth = proxy_weight.shape[0]
    total_d, total_p = rows * n_fsdp, width * n_tp
    far = keeps[-1]

    w = gather_blocks(grow_operator, n_fsdp, bits)
    r = gather_blocks(after(proxy_weight, w[far]), n_fsdp, bits)

    keep_mask = (jnp.arange(LEN, dtype=jnp.int32)[None, :] < lengths[:, None]).reshape(-1)
    grad_rows = jnp.where(keep_mask[:, None], cotangent, jnp.zeros_like(cotangent))

    def in_order(value):
        return jnp.concatenate(
            [lax.dynamic_slice_in_dim(value, (me ^ m) * rows, rows, axis=1) for m in order], axis=1
        )

    both = jnp.concatenate([in_order(activations), in_order(grad_rows)], axis=0)

    acc = None
    for mask in sorted(order, key=lambda m: (bin(m >> 1).count("1"), m & 1, m)):
        place = order.index(mask) * rows
        part = dot(both[:, place : place + rows], w[mask], (1, 0))
        acc = part if acc is None else acc + part
    forward = acc[:tokens].astype(BF)
    back = acc[tokens:].astype(BF)

    proxy = jnp.zeros((total_p, width), BF)
    for mask in order:
        proxy = lax.dynamic_update_slice_in_dim(proxy, r[mask], (me ^ mask) * depth, axis=0)

    ups = [(i, i + 1) for i in range(n_tp - 1)]
    downs = [(i + 1, i) for i in range(n_tp - 1)]
    from_low, from_high = [back], [back]
    for _ in range(n_tp - 1):
        from_low.append(lax.ppermute(from_low[-1], "tp", ups))
        from_high.append(lax.ppermute(from_high[-1], "tp", downs))
    back_all = jnp.zeros((tokens, total_p), BF)
    back_all = lax.dynamic_update_slice_in_dim(back_all, back, at * width, axis=1)
    for hop in range(1, n_tp):
        piece = from_low[hop] + from_high[n_tp - hop]
        where = lax.rem(at - hop + n_tp, n_tp) * width
        back_all = lax.dynamic_update_slice_in_dim(back_all, piece, where, axis=1)

    step = width // CHUNKS
    squares = jnp.zeros((), F32)
    pieces = []
    for c in range(CHUNKS):
        def partial(owner):
            start = jnp.clip(owner, 0, n_tp - 1) * width + c * step
            return dot(forward, lax.dynamic_slice_in_dim(proxy, start, step, axis=0), (1, 1))

        up = down = None
        for hop in range(1, n_tp):
            send_up = partial(n_tp - hop + at)
            send_down = partial(at + hop - n_tp)
            if up is not None:
                send_up, send_down = send_up + up, send_down + down
            up = lax.ppermute(send_up.astype(BF), "tp", [(i, i + 1) for i in range(hop)])
            down = lax.ppermute(
                send_down.astype(BF), "tp", [(n_tp - 1 - i, n_tp - 2 - i) for i in range(hop)]
            )
        proxy_out = partial(at)
        if up is not None:
            proxy_out = proxy_out + up.astype(F32) + down.astype(F32)
        delta = dot(back_all, proxy[:, c * step : (c + 1) * step], (1, 0))
        values = jnp.concatenate([delta.astype(BF), proxy_out.astype(BF)], axis=0)

        half = rows * len(keeps)
        send = dot(both[:, half:], values, (0, 0)).astype(BF)
        arrived = flip(send, "fsdp", n_fsdp, 1)
        pair = (dot(both[:, :half], values, (0, 0)) + arrived.astype(F32)).astype(BF)
        pair = pair.reshape(len(keeps), rows, step)
        for number, sequence in enumerate((bits, bits[::-1])):
            lo = number * (step // 2)
            held = {m: pair[i, :, lo : lo + step // 2].astype(F32) for i, m in enumerate(keeps)}
            for bit in sequence:
                leaving = [m for m in held if m & bit]
                packed = jnp.stack([held[m].astype(BF) for m in leaving])
                packed = flip(packed, "fsdp", n_fsdp, bit)
                for i, m in enumerate(leaving):
                    held[m ^ bit] = held[m ^ bit] + packed[i].astype(F32)
                    del held[m]
            pieces.append(held[0])
            squares = squares + jnp.sum(held[0] * held[0])

    total = jnp.broadcast_to(squares, (8, 128))
    for axis, size in (("fsdp", n_fsdp), ("tp", n_tp)):
        bit = 1
        while bit < size:
            total = total + flip(total, axis, size, bit)
            bit *= 2
    mean_sq = total[0, 0] / (total_d * total_p)
    scale = lax.rsqrt(mean_sq + 1e-06)
    return jnp.concatenate([(piece * scale).astype(BF) for piece in pieces], axis=1)


def solution(mesh):
    n_fsdp, n_tp = mesh.shape["fsdp"], mesh.shape["tp"]
    placed = (P("fsdp", None), P("fsdp", None), P("fsdp"), P("fsdp", "tp"), P("fsdp", "tp"))

    def body(*args):
        return per_device(n_fsdp, n_tp, *args)

    return jax.shard_map(
        body, mesh=mesh, in_specs=placed, out_specs=P("fsdp", "tp"), check_vma=False
    )
```

```python
import jax
import jax.numpy as jnp
from jax import lax
from jax.experimental import pallas as pl
from jax.experimental.pallas import tpu as pltpu
from jax.sharding import PartitionSpec as P


LEN = 256
CHUNKS = 2
BF = jnp.bfloat16
F32 = jnp.float32


def dot(left, right, dims):
    return lax.dot_general(left, right, ((dims[:1], dims[1:]), ((), ())), preferred_element_type=F32)


def flip(value, axis, size, bit):
    return lax.ppermute(value, axis, [(i, i ^ bit) for i in range(size)])


def after(value, *others):
    return lax.optimization_barrier((value,) + others)[0]


def masks_of(bits):
    masks = [0]
    for bit in bits:
        masks = masks + [m | bit for m in masks]
    return sorted(masks, key=lambda m: (bin(m).count("1"), m))


def gather_blocks(shard, size, bits, ends):
    got = {0: shard}
    half = shard.shape[0] // 2
    for mask in masks_of(bits)[1:]:
        inside = [bit for bit in bits if mask & bit]
        if len(inside) == 1:
            got[mask] = flip(shard, "fsdp", size, inside[0])
        else:
            first, last = inside[0], inside[-1]
            low = flip(got[mask ^ last][:half], "fsdp", size, last)
            high = flip(got[mask ^ first][half:], "fsdp", size, first)
            got[mask] = jnp.concatenate([low, high], axis=0)
            ends[:] = [low, high]
    for mask in masks_of(bits):
        got[mask ^ 1] = flip(got[mask], "fsdp", size, 1)
    return got


def order_kernel(places, lengths, act_ref, cot_ref, out_ref):
    tokens = act_ref.shape[0]
    out_ref[:tokens, :] = act_ref[...]
    position = lax.broadcasted_iota(jnp.int32, (LEN, act_ref.shape[1]), 0)
    for i in range(tokens // LEN):
        rows = cot_ref[i * LEN : (i + 1) * LEN, :]
        kept = jnp.where(position < lengths[i], rows, jnp.zeros_like(rows))
        out_ref[tokens + i * LEN : tokens + (i + 1) * LEN, :] = kept


def ordered(places, lengths, activations, cotangent, cols):
    tokens, total = activations.shape
    if cols % 128:
        keep = (jnp.arange(LEN, dtype=jnp.int32)[None, :] < lengths[:, None]).reshape(-1)
        kept = jnp.where(keep[:, None], cotangent, jnp.zeros_like(cotangent))
        both = jnp.concatenate([activations, kept], axis=0)
        return jnp.concatenate(
            [lax.dynamic_slice_in_dim(both, p * cols, cols, axis=1) for p in places], axis=1
        )
    block = pl.BlockSpec((tokens, cols), lambda m, where, _: (0, where[m]))
    return pl.pallas_call(
        order_kernel,
        out_shape=jax.ShapeDtypeStruct((2 * tokens, total), activations.dtype),
        grid_spec=pltpu.PrefetchScalarGridSpec(
            num_scalar_prefetch=2,
            grid=(total // cols,),
            in_specs=[block, block],
            out_specs=pl.BlockSpec((2 * tokens, cols), lambda m, where, _: (0, m)),
        ),
        compiler_params=pltpu.CompilerParams(vmem_limit_bytes=24 << 20),
        cost_estimate=pl.CostEstimate(flops=0, bytes_accessed=8 * tokens * total, transcendentals=0),
    )(jnp.stack(places), lengths, activations, cotangent)


def per_device(n_fsdp, n_tp, activations, cotangent, lengths, grow_operator, proxy_weight):
    me = lax.axis_index("fsdp")
    at = lax.axis_index("tp")
    bits = []
    while 2 << len(bits) < n_fsdp:
        bits.append(2 << len(bits))
    keeps = masks_of(bits)
    order = keeps + [m ^ 1 for m in keeps]
    tokens = activations.shape[0]
    rows, width = grow_operator.shape
    depth = proxy_weight.shape[0]
    total_d, total_p = rows * n_fsdp, width * n_tp

    ends = []
    w = gather_blocks(grow_operator, n_fsdp, bits, ends)
    r = gather_blocks(after(proxy_weight, *ends), n_fsdp, bits, ends)

    both = ordered([me ^ m for m in order], lengths, activations, cotangent, rows)

    acc = None
    for mask in sorted(order, key=lambda m: (bin(m >> 1).count("1"), m & 1, m)):
        place = order.index(mask) * rows
        part = dot(both[:, place : place + rows], w[mask], (1, 0))
        acc = part if acc is None else acc + part
    forward = acc[:tokens].astype(BF)
    back = acc[tokens:].astype(BF)

    proxy = jnp.zeros((total_p, width), BF)
    for mask in order:
        proxy = lax.dynamic_update_slice_in_dim(proxy, r[mask], (me ^ mask) * depth, axis=0)

    ups = [(i, i + 1) for i in range(n_tp - 1)]
    downs = [(i + 1, i) for i in range(n_tp - 1)]
    from_low, from_high = [back], [back]
    for _ in range(n_tp - 1):
        from_low.append(lax.ppermute(from_low[-1], "tp", ups))
        from_high.append(lax.ppermute(from_high[-1], "tp", downs))
    back_all = jnp.zeros((tokens, total_p), BF)
    back_all = lax.dynamic_update_slice_in_dim(back_all, back, at * width, axis=1)
    for hop in range(1, n_tp):
        piece = from_low[hop] + from_high[n_tp - hop]
        where = lax.rem(at - hop + n_tp, n_tp) * width
        back_all = lax.dynamic_update_slice_in_dim(back_all, piece, where, axis=1)

    forward = after(forward, from_low[1], from_high[1])

    step = width // CHUNKS
    squares = jnp.zeros((), F32)
    pieces = []
    for c in range(CHUNKS):
        def partial(owner):
            start = jnp.clip(owner, 0, n_tp - 1) * width + c * step
            return dot(forward, lax.dynamic_slice_in_dim(proxy, start, step, axis=0), (1, 1))

        up = down = None
        for hop in range(1, n_tp):
            send_up = partial(n_tp - hop + at)
            send_down = partial(at + hop - n_tp)
            if up is not None:
                up, down = after(up, from_low[hop]), after(down, from_high[hop])
                send_up, send_down = send_up + up, send_down + down
            up = lax.ppermute(send_up.astype(BF), "tp", [(i, i + 1) for i in range(hop)])
            down = lax.ppermute(
                send_down.astype(BF), "tp", [(n_tp - 1 - i, n_tp - 2 - i) for i in range(hop)]
            )
        proxy_out = partial(at)
        if up is not None:
            proxy_out = proxy_out + up.astype(F32) + down.astype(F32)
        delta = dot(back_all, proxy[:, c * step : (c + 1) * step], (1, 0))
        values = jnp.concatenate([delta.astype(BF), proxy_out.astype(BF)], axis=0)

        half = rows * len(keeps)
        send = dot(both[:, half:], values, (0, 0)).astype(BF)
        arrived = flip(send, "fsdp", n_fsdp, 1)
        pair = (dot(both[:, :half], values, (0, 0)) + arrived.astype(F32)).astype(BF)
        pair = pair.reshape(len(keeps), rows, step)
        for number, sequence in enumerate((bits, bits[::-1])):
            lo = number * (step // 2)
            held = {m: pair[i, :, lo : lo + step // 2].astype(F32) for i, m in enumerate(keeps)}
            for bit in sequence:
                leaving = [m for m in held if m & bit]
                packed = jnp.stack([held[m].astype(BF) for m in leaving])
                packed = flip(packed, "fsdp", n_fsdp, bit)
                for i, m in enumerate(leaving):
                    held[m ^ bit] = held[m ^ bit] + packed[i].astype(F32)
                    del held[m]
            pieces.append(held[0])
            squares = squares + jnp.sum(held[0] * held[0])

    total = jnp.broadcast_to(squares, (8, 128))
    for axis, size in (("fsdp", n_fsdp), ("tp", n_tp)):
        bit = 1
        while bit < size:
            total = total + flip(total, axis, size, bit)
            bit *= 2
    mean_sq = total[0, 0] / (total_d * total_p)
    scale = lax.rsqrt(mean_sq + 1e-06)
    return jnp.concatenate([(piece * scale).astype(BF) for piece in pieces], axis=1)


def solution(mesh):
    n_fsdp, n_tp = mesh.shape["fsdp"], mesh.shape["tp"]
    placed = (P("fsdp", None), P("fsdp", None), P("fsdp"), P("fsdp", "tp"), P("fsdp", "tp"))

    def body(*args):
        return per_device(n_fsdp, n_tp, *args)

    return jax.shard_map(
        body, mesh=mesh, in_specs=placed, out_specs=P("fsdp", "tp"), check_vma=False
    )
```

```python
import jax
import jax.numpy as jnp
from jax import lax
from jax.experimental import pallas as pl
from jax.experimental.pallas import tpu as pltpu
from jax.sharding import PartitionSpec as P


LEN = 256
BF = jnp.bfloat16
F32 = jnp.float32


def dot(left, right, dims):
    return lax.dot_general(left, right, ((dims[:1], dims[1:]), ((), ())), preferred_element_type=F32)


def flip(value, axis, size, bit):
    return lax.ppermute(value, axis, [(i, i ^ bit) for i in range(size)])


def after(value, *others):
    return lax.optimization_barrier((value,) + others)[0]


def masks_of(bits):
    masks = [0]
    for bit in bits:
        masks = masks + [m | bit for m in masks]
    return sorted(masks, key=lambda m: (bin(m).count("1"), m))


def gather_near(shard, size, bits):
    return {0: shard, **{bit: flip(shard, "fsdp", size, bit) for bit in bits}}


def gather_far(got, size, bits, gate):
    got = {m: after(block, gate) for m, block in got.items()}
    half = got[0].shape[0] // 2
    low = high = None
    for mask in masks_of(bits)[1 + len(bits) :]:
        inside = [bit for bit in bits if mask & bit]
        first, last = inside[0], inside[-1]
        low = flip(got[mask ^ last][:half], "fsdp", size, last)
        high = flip(got[mask ^ first][half:], "fsdp", size, first)
        got[mask] = jnp.concatenate([low, high], axis=0)
    for mask in masks_of(bits):
        got[mask ^ 1] = flip(got[mask], "fsdp", size, 1)
    return got, (low, high)


def order_kernel(places, lengths, act_ref, cot_ref, out_ref):
    tokens = act_ref.shape[0]
    out_ref[:tokens, :] = act_ref[...]
    position = lax.broadcasted_iota(jnp.int32, (LEN, act_ref.shape[1]), 0)
    for i in range(tokens // LEN):
        rows = cot_ref[i * LEN : (i + 1) * LEN, :]
        kept = jnp.where(position < lengths[i], rows, jnp.zeros_like(rows))
        out_ref[tokens + i * LEN : tokens + (i + 1) * LEN, :] = kept


def ordered(places, lengths, activations, cotangent, cols):
    tokens, total = activations.shape
    if cols % 128:
        keep = (jnp.arange(LEN, dtype=jnp.int32)[None, :] < lengths[:, None]).reshape(-1)
        kept = jnp.where(keep[:, None], cotangent, jnp.zeros_like(cotangent))
        both = jnp.concatenate([activations, kept], axis=0)
        return jnp.concatenate(
            [lax.dynamic_slice_in_dim(both, p * cols, cols, axis=1) for p in places], axis=1
        )
    block = pl.BlockSpec((tokens, cols), lambda m, where, _: (0, where[m]))
    return pl.pallas_call(
        order_kernel,
        out_shape=jax.ShapeDtypeStruct((2 * tokens, total), activations.dtype),
        grid_spec=pltpu.PrefetchScalarGridSpec(
            num_scalar_prefetch=2,
            grid=(total // cols,),
            in_specs=[block, block],
            out_specs=pl.BlockSpec((2 * tokens, cols), lambda m, where, _: (0, m)),
        ),
        compiler_params=pltpu.CompilerParams(vmem_limit_bytes=24 << 20),
        cost_estimate=pl.CostEstimate(flops=0, bytes_accessed=8 * tokens * total, transcendentals=0),
    )(jnp.stack(places), lengths, activations, cotangent)


def per_device(n_fsdp, n_tp, activations, cotangent, lengths, grow_operator, proxy_weight):
    me = lax.axis_index("fsdp")
    at = lax.axis_index("tp")
    bits = []
    while 2 << len(bits) < n_fsdp:
        bits.append(2 << len(bits))
    keeps = masks_of(bits)
    near, far = keeps[:-1], keeps[-1]
    order = near + [m ^ 1 for m in near] + [far, far ^ 1]
    tokens = activations.shape[0]
    rows, width = grow_operator.shape
    split = 2 * len(near) * rows
    depth = proxy_weight.shape[0]
    total_d, total_p = rows * n_fsdp, width * n_tp

    both = ordered([me ^ m for m in order], lengths, activations, cotangent, rows)

    w = gather_near(grow_operator, n_fsdp, bits)
    w, ends = gather_far(w, n_fsdp, bits, both)
    r = gather_near(after(proxy_weight, *ends), n_fsdp, bits)

    acc = dot(both[:, :split], jnp.concatenate([w[m] for m in order[:-2]], axis=0), (1, 0))
    acc = acc + dot(both[:, split:], jnp.concatenate([w[far], w[far ^ 1]], axis=0), (1, 0))
    forward = acc[:tokens].astype(BF)
    back = acc[tokens:].astype(BF)

    r, _ = gather_far(r, n_fsdp, bits, forward)

    chunks = width // depth
    proxy = jnp.zeros((total_p, width), BF)
    for mask in order:
        owner = me ^ mask
        row = (lax.rem(owner, chunks) * n_tp + owner // chunks) * depth
        proxy = lax.dynamic_update_slice_in_dim(proxy, r[mask], row, axis=0)

    ups = [(i, i + 1) for i in range(n_tp - 1)]
    downs = [(i + 1, i) for i in range(n_tp - 1)]
    from_low, from_high = [back], [back]
    for _ in range(n_tp - 1):
        from_low.append(lax.ppermute(from_low[-1], "tp", ups))
        from_high.append(lax.ppermute(from_high[-1], "tp", downs))
    back_all = jnp.zeros((tokens, total_p), BF)
    for hop in range(n_tp):
        piece = from_low[hop] + from_high[n_tp - hop] if hop else back
        owner = lax.rem(at - hop + n_tp, n_tp)
        for c in range(chunks):
            part = piece[:, c * depth : (c + 1) * depth]
            column = (c * n_tp + owner) * depth
            back_all = lax.dynamic_update_slice_in_dim(back_all, part, column, axis=1)

    step = depth
    group = n_tp * depth
    squares = jnp.zeros((), F32)
    pieces = []
    sent = None
    for c in range(chunks):
        hop = min(c + 1, n_tp - 1)
        forward = after(forward, from_low[hop], from_high[hop])
        partial = dot(forward, proxy[c * group : (c + 1) * group], (1, 1)).astype(BF)
        proxy_out = lax.psum_scatter(partial, "tp", scatter_dimension=1, tiled=True)
        if sent is not None:
            proxy_out = after(proxy_out, *sent)
        delta = dot(back_all, proxy[:, c * step : (c + 1) * step], (1, 0))
        values = jnp.concatenate([delta.astype(BF), proxy_out], axis=0)

        half = split // 2
        blocks = {}
        for lo, mid, hi, masks in ((0, half, split, near), (split, split + rows, split + 2 * rows, [far])):
            send = dot(both[:, mid:hi], values, (0, 0)).astype(BF)
            arrived = flip(send, "fsdp", n_fsdp, 1)
            pair = (dot(both[:, lo:mid], values, (0, 0)) + arrived.astype(F32)).astype(BF)
            for i, m in enumerate(masks):
                blocks[m] = pair[i * rows : (i + 1) * rows]
        sent = []
        for number, sequence in enumerate((bits, bits[::-1])):
            lo = number * (step // 2)
            held = {m: blocks[m][:, lo : lo + step // 2].astype(F32) for m in keeps}
            for bit in sequence:
                leaving = [m for m in held if m & bit]
                packed = jnp.stack([held[m].astype(BF) for m in leaving])
                packed = flip(packed, "fsdp", n_fsdp, bit)
                if bit != sequence[-1] or len(sequence) == 1:
                    sent.append(packed)
                for i, m in enumerate(leaving):
                    held[m ^ bit] = held[m ^ bit] + packed[i].astype(F32)
                    del held[m]
            pieces.append(held[0])
            squares = squares + jnp.sum(held[0] * held[0])

    total = jnp.broadcast_to(squares, (8, 128))
    for axis, size in (("fsdp", n_fsdp), ("tp", n_tp)):
        bit = 1
        while bit < size:
            total = total + flip(total, axis, size, bit)
            bit *= 2
    mean_sq = total[0, 0] / (total_d * total_p)
    scale = lax.rsqrt(mean_sq + 1e-06)
    return jnp.concatenate([(piece * scale).astype(BF) for piece in pieces], axis=1)


def solution(mesh):
    n_fsdp, n_tp = mesh.shape["fsdp"], mesh.shape["tp"]
    placed = (P("fsdp", None), P("fsdp", None), P("fsdp"), P("fsdp", "tp"), P("fsdp", "tp"))

    def body(*args):
        return per_device(n_fsdp, n_tp, *args)

    return jax.shard_map(
        body, mesh=mesh, in_specs=placed, out_specs=P("fsdp", "tp"), check_vma=False
    )
```

```python
import jax
import jax.numpy as jnp
from jax import lax
from jax.experimental import pallas as pl
from jax.experimental.pallas import tpu as pltpu
from jax.sharding import PartitionSpec as P


LEN = 256
BF = jnp.bfloat16
F32 = jnp.float32


def dot(left, right, dims):
    return lax.dot_general(left, right, ((dims[:1], dims[1:]), ((), ())), preferred_element_type=F32)


def flip(value, axis, size, bit):
    return lax.ppermute(value, axis, [(i, i ^ bit) for i in range(size)])


def after(value, *others):
    return lax.optimization_barrier((value,) + others)[0]


def masks_of(bits):
    masks = [0]
    for bit in bits:
        masks = masks + [m | bit for m in masks]
    return sorted(masks, key=lambda m: (bin(m).count("1"), m))


def gather_near(shard, size, bits):
    return {0: shard, **{bit: flip(shard, "fsdp", size, bit) for bit in bits}}


def gather_far(got, size, bits, gate):
    got = {m: after(block, gate) for m, block in got.items()}
    half = got[0].shape[0] // 2
    low = high = None
    for mask in masks_of(bits)[1 + len(bits) :]:
        inside = [bit for bit in bits if mask & bit]
        first, last = inside[0], inside[-1]
        low = flip(got[mask ^ last][:half], "fsdp", size, last)
        high = flip(got[mask ^ first][half:], "fsdp", size, first)
        got[mask] = jnp.concatenate([low, high], axis=0)
    for mask in masks_of(bits):
        got[mask ^ 1] = flip(got[mask], "fsdp", size, 1)
    return got, (low, high)


def order_kernel(places, lengths, act_ref, cot_ref, out_ref):
    tokens = act_ref.shape[0]
    out_ref[:tokens, :] = act_ref[...]
    position = lax.broadcasted_iota(jnp.int32, (LEN, act_ref.shape[1]), 0)
    for i in range(tokens // LEN):
        rows = cot_ref[i * LEN : (i + 1) * LEN, :]
        kept = jnp.where(position < lengths[i], rows, jnp.zeros_like(rows))
        out_ref[tokens + i * LEN : tokens + (i + 1) * LEN, :] = kept


def ordered(places, lengths, activations, cotangent, cols):
    tokens, total = activations.shape
    if cols % 128:
        keep = (jnp.arange(LEN, dtype=jnp.int32)[None, :] < lengths[:, None]).reshape(-1)
        kept = jnp.where(keep[:, None], cotangent, jnp.zeros_like(cotangent))
        both = jnp.concatenate([activations, kept], axis=0)
        return jnp.concatenate(
            [lax.dynamic_slice_in_dim(both, p * cols, cols, axis=1) for p in places], axis=1
        )
    block = pl.BlockSpec((tokens, cols), lambda m, where, _: (0, where[m]))
    return pl.pallas_call(
        order_kernel,
        out_shape=jax.ShapeDtypeStruct((2 * tokens, total), activations.dtype),
        grid_spec=pltpu.PrefetchScalarGridSpec(
            num_scalar_prefetch=2,
            grid=(total // cols,),
            in_specs=[block, block],
            out_specs=pl.BlockSpec((2 * tokens, cols), lambda m, where, _: (0, m)),
        ),
        compiler_params=pltpu.CompilerParams(vmem_limit_bytes=24 << 20),
        cost_estimate=pl.CostEstimate(flops=0, bytes_accessed=8 * tokens * total, transcendentals=0),
    )(jnp.stack(places), lengths, activations, cotangent)


def per_device(n_fsdp, n_tp, activations, cotangent, lengths, grow_operator, proxy_weight):
    me = lax.axis_index("fsdp")
    at = lax.axis_index("tp")
    bits = []
    while 2 << len(bits) < n_fsdp:
        bits.append(2 << len(bits))
    keeps = masks_of(bits)
    order = keeps + [m ^ 1 for m in keeps]
    tokens = activations.shape[0]
    rows, width = grow_operator.shape
    split = len(keeps) * rows
    depth = proxy_weight.shape[0]
    total_d, total_p = rows * n_fsdp, width * n_tp

    both = ordered([me ^ m for m in order], lengths, activations, cotangent, rows)

    w = gather_near(grow_operator, n_fsdp, bits)
    w, ends = gather_far(w, n_fsdp, bits, both)
    r = gather_near(after(proxy_weight, *ends), n_fsdp, bits)

    acc = dot(both, jnp.concatenate([w[m] for m in order], axis=0), (1, 0))
    forward = acc[:tokens].astype(BF)
    back = acc[tokens:].astype(BF)

    r, _ = gather_far(r, n_fsdp, bits, forward)

    chunks = width // depth
    proxy = jnp.zeros((total_p, width), BF)
    for mask in order:
        owner = me ^ mask
        row = (lax.rem(owner, chunks) * n_tp + owner // chunks) * depth
        proxy = lax.dynamic_update_slice_in_dim(proxy, r[mask], row, axis=0)

    last = n_tp - 1
    from_low, from_high = [back], [back]
    for hop in range(last):
        from_low.append(lax.ppermute(from_low[-1], "tp", [(i, i + 1) for i in range(hop, last)]))
        from_high.append(
            lax.ppermute(from_high[-1], "tp", [(last - i, last - 1 - i) for i in range(hop, last)])
        )
    back_all = jnp.zeros((tokens, total_p), BF)
    for hop in range(n_tp):
        piece = from_low[hop] + from_high[n_tp - hop] if hop else back
        owner = lax.rem(at - hop + n_tp, n_tp)
        for c in range(chunks):
            part = piece[:, c * depth : (c + 1) * depth]
            column = (c * n_tp + owner) * depth
            back_all = lax.dynamic_update_slice_in_dim(back_all, part, column, axis=1)

    step = depth
    forward = after(forward, from_low[1], from_high[1])

    sums, own = [], []
    for c in range(chunks):
        group = n_tp * depth
        partials = dot(forward, proxy[c * group : (c + 1) * group], (1, 1))

        def partial(owner):
            column = jnp.clip(owner, 0, last) * depth
            return lax.dynamic_slice_in_dim(partials, column, depth, axis=1)

        ups, downs, up, down = [], [], None, None
        for hop in range(1, n_tp):
            send_up, send_down = partial(n_tp - hop + at), partial(at + hop - n_tp)
            if up is not None:
                send_up, send_down = send_up + up, send_down + down
            send_up, send_down = send_up.astype(BF), send_down.astype(BF)
            if hop == 1 and c:
                send_up, send_down = after(send_up, *sums[-1][0]), after(send_down, *sums[-1][0])
            if hop == last:
                send_up, send_down = after(send_up, from_low[2]), after(send_down, from_high[2])
            up = lax.ppermute(send_up, "tp", [(i, i + 1) for i in range(hop)])
            down = lax.ppermute(send_down, "tp", [(last - i, last - 1 - i) for i in range(hop)])
            ups.append(up)
            downs.append(down)
        sums.append(list(zip(ups, downs)))
        own.append(partial(at))

    squares = jnp.zeros((), F32)
    pieces = []
    sent = None
    for c in range(chunks):
        up, down = sums[c][-1]
        if c + 1 < chunks:
            up, down = after(up, *sums[c + 1][-2]), after(down, *sums[c + 1][-2])
        if sent is not None:
            up, down = after(up, *sent), after(down, *sent)
        proxy_out = (own[c] + up.astype(F32) + down.astype(F32)).astype(BF)
        delta = dot(back_all, proxy[:, c * step : (c + 1) * step], (1, 0))
        values = jnp.concatenate([delta.astype(BF), proxy_out], axis=0)

        send = dot(both[:, split:], values, (0, 0)).astype(BF)
        arrived = flip(send, "fsdp", n_fsdp, 1)
        pair = (dot(both[:, :split], values, (0, 0)) + arrived.astype(F32)).astype(BF)
        blocks = {m: pair[i * rows : (i + 1) * rows] for i, m in enumerate(keeps)}
        sent = []
        for number, sequence in enumerate((bits, bits[::-1])):
            lo = number * (step // 2)
            held = {m: blocks[m][:, lo : lo + step // 2].astype(F32) for m in keeps}
            for bit in sequence:
                leaving = [m for m in held if m & bit]
                packed = jnp.stack([held[m].astype(BF) for m in leaving])
                packed = flip(packed, "fsdp", n_fsdp, bit)
                if bit != sequence[-1] or len(sequence) == 1:
                    sent.append(packed)
                for i, m in enumerate(leaving):
                    held[m ^ bit] = held[m ^ bit] + packed[i].astype(F32)
                    del held[m]
            pieces.append(held[0])
            squares = squares + jnp.sum(held[0] * held[0])

    total = jnp.broadcast_to(squares, (8, 128))
    total = total + flip(total, "fsdp", n_fsdp, 1)
    total = total + sum(flip(total, "fsdp", n_fsdp, m) for m in keeps[1:])
    total = total + sum(
        lax.ppermute(total, "tp", [(i, (i + k) % n_tp) for i in range(n_tp)]) for k in range(1, n_tp)
    )
    mean_sq = total[0, 0] / (total_d * total_p)
    scale = lax.rsqrt(mean_sq + 1e-06)
    return jnp.concatenate([(piece * scale).astype(BF) for piece in pieces], axis=1)


def solution(mesh):
    n_fsdp, n_tp = mesh.shape["fsdp"], mesh.shape["tp"]
    placed = (P("fsdp", None), P("fsdp", None), P("fsdp"), P("fsdp", "tp"), P("fsdp", "tp"))

    def body(*args):
        return per_device(n_fsdp, n_tp, *args)

    return jax.shard_map(
        body, mesh=mesh, in_specs=placed, out_specs=P("fsdp", "tp"), check_vma=False
    )
```

```python
import jax
import jax.numpy as jnp
from jax import lax
from jax.experimental import pallas as pl
from jax.experimental.pallas import tpu as pltpu
from jax.sharding import PartitionSpec as P


LEN = 256
BF = jnp.bfloat16
F32 = jnp.float32


def dot(left, right, dims):
    return lax.dot_general(left, right, ((dims[:1], dims[1:]), ((), ())), preferred_element_type=F32)


def flip(value, axis, size, bit):
    return lax.ppermute(value, axis, [(i, i ^ bit) for i in range(size)])


def after(value, *others):
    return lax.optimization_barrier((value,) + others)[0]


def masks_of(bits):
    masks = [0]
    for bit in bits:
        masks = masks + [m | bit for m in masks]
    return sorted(masks, key=lambda m: (bin(m).count("1"), m))


def gather_near(shard, size, bits):
    return {0: shard, **{bit: flip(shard, "fsdp", size, bit) for bit in bits}}


def gather_far(got, size, bits, gate):
    got = {m: after(block, gate) for m, block in got.items()}
    half = got[0].shape[0] // 2
    low = high = None
    for mask in masks_of(bits)[1 + len(bits) :]:
        inside = [bit for bit in bits if mask & bit]
        first, last = inside[0], inside[-1]
        low, high = got[mask ^ last][:half], got[mask ^ first][half:]
        low, high = flip(low, "fsdp", size, last), flip(high, "fsdp", size, first)
        got[mask] = jnp.concatenate([low, high], axis=0)
    for mask in masks_of(bits):
        got[mask ^ 1] = flip(got[mask], "fsdp", size, 1)
    return got, (low, high)


def order_kernel(places, lengths, act_ref, cot_ref, out_ref):
    tokens = act_ref.shape[0]
    out_ref[:tokens, :] = act_ref[...]
    position = lax.broadcasted_iota(jnp.int32, (LEN, act_ref.shape[1]), 0)
    for i in range(tokens // LEN):
        rows = cot_ref[i * LEN : (i + 1) * LEN, :]
        kept = jnp.where(position < lengths[i], rows, jnp.zeros_like(rows))
        out_ref[tokens + i * LEN : tokens + (i + 1) * LEN, :] = kept


def ordered(places, lengths, activations, cotangent, cols):
    tokens, total = activations.shape
    if cols % 128:
        keep = (jnp.arange(LEN, dtype=jnp.int32)[None, :] < lengths[:, None]).reshape(-1)
        kept = jnp.where(keep[:, None], cotangent, jnp.zeros_like(cotangent))
        both = jnp.concatenate([activations, kept], axis=0)
        return jnp.concatenate(
            [lax.dynamic_slice_in_dim(both, p * cols, cols, axis=1) for p in places], axis=1
        )
    block = pl.BlockSpec((tokens, cols), lambda m, where, _: (0, where[m]))
    return pl.pallas_call(
        order_kernel,
        out_shape=jax.ShapeDtypeStruct((2 * tokens, total), activations.dtype),
        grid_spec=pltpu.PrefetchScalarGridSpec(
            num_scalar_prefetch=2,
            grid=(total // cols,),
            in_specs=[block, block],
            out_specs=pl.BlockSpec((2 * tokens, cols), lambda m, where, _: (0, m)),
        ),
        compiler_params=pltpu.CompilerParams(vmem_limit_bytes=24 << 20),
        cost_estimate=pl.CostEstimate(flops=0, bytes_accessed=8 * tokens * total, transcendentals=0),
    )(jnp.stack(places), lengths, activations, cotangent)


def per_device(n_fsdp, n_tp, activations, cotangent, lengths, grow_operator, proxy_weight):
    me = lax.axis_index("fsdp")
    at = lax.axis_index("tp")
    bits = []
    while 2 << len(bits) < n_fsdp:
        bits.append(2 << len(bits))
    keeps = masks_of(bits)
    order = keeps + [m ^ 1 for m in keeps]
    tokens = activations.shape[0]
    rows, width = grow_operator.shape
    split = len(keeps) * rows
    depth = proxy_weight.shape[0]
    total_d, total_p = rows * n_fsdp, width * n_tp

    both = ordered([me ^ m for m in order], lengths, activations, cotangent, rows)

    w = gather_near(grow_operator, n_fsdp, bits)
    w, ends = gather_far(w, n_fsdp, bits, both)
    r = gather_near(after(proxy_weight, *ends), n_fsdp, bits)

    acc = dot(both, jnp.concatenate([w[m] for m in order], axis=0), (1, 0))
    forward = acc[:tokens].astype(BF)
    back = acc[tokens:].astype(BF)

    r, _ = gather_far(r, n_fsdp, bits, forward)

    chunks = width // depth
    proxy = jnp.zeros((total_p, width), BF)
    for mask in order:
        owner = me ^ mask
        row = (lax.rem(owner, chunks) * n_tp + owner // chunks) * depth
        proxy = lax.dynamic_update_slice_in_dim(proxy, r[mask], row, axis=0)

    last = n_tp - 1
    from_low, from_high = [back], [back]
    for hop in range(last):
        pairs = [(i, i + 1) for i in range(hop, last)]
        from_low.append(lax.ppermute(from_low[-1], "tp", pairs))
        pairs = [(last - i, last - 1 - i) for i in range(hop, last)]
        from_high.append(lax.ppermute(from_high[-1], "tp", pairs))
    back_all = jnp.zeros((tokens, total_p), BF)
    for hop in range(n_tp):
        piece = from_low[hop] + from_high[n_tp - hop] if hop else back
        owner = lax.rem(at - hop + n_tp, n_tp)
        for c in range(chunks):
            part = piece[:, c * depth : (c + 1) * depth]
            column = (c * n_tp + owner) * depth
            back_all = lax.dynamic_update_slice_in_dim(back_all, part, column, axis=1)

    step = depth
    forward = after(forward, from_low[1], from_high[1])

    sums, own = [], []
    for c in range(chunks):
        group = n_tp * depth
        partials = dot(forward, proxy[c * group : (c + 1) * group], (1, 1))

        def partial(owner):
            column = jnp.clip(owner, 0, last) * depth
            return lax.dynamic_slice_in_dim(partials, column, depth, axis=1)

        ups, downs, up, down = [], [], None, None
        for hop in range(1, n_tp):
            send_up, send_down = partial(n_tp - hop + at), partial(at + hop - n_tp)
            if up is not None:
                send_up, send_down = send_up + up, send_down + down
            send_up, send_down = send_up.astype(BF), send_down.astype(BF)
            if hop == 1 and c:
                send_up, send_down = after(send_up, *sums[-1][0]), after(send_down, *sums[-1][0])
            if hop == last:
                send_up, send_down = after(send_up, from_low[2]), after(send_down, from_high[2])
            up = lax.ppermute(send_up, "tp", [(i, i + 1) for i in range(hop)])
            down = lax.ppermute(send_down, "tp", [(last - i, last - 1 - i) for i in range(hop)])
            ups.append(up)
            downs.append(down)
        sums.append(list(zip(ups, downs)))
        own.append(partial(at))

    squares = jnp.zeros((), F32)
    pieces = []
    for c in range(chunks):
        up, down = sums[c][-1]
        if c + 1 < chunks:
            up, down = after(up, *sums[c + 1][-2]), after(down, *sums[c + 1][-2])
        proxy_out = (own[c] + up.astype(F32) + down.astype(F32)).astype(BF)
        delta = dot(back_all, proxy[:, c * step : (c + 1) * step], (1, 0))
        values = jnp.concatenate([delta.astype(BF), proxy_out], axis=0)

        send = dot(both[:, split:], values, (0, 0)).astype(BF)
        arrived = flip(send, "fsdp", n_fsdp, 1)
        keep = after(dot(both[:, :split], values, (0, 0)), values)
        pair = (keep + arrived.astype(F32)).astype(BF)
        blocks = {m: pair[i * rows : (i + 1) * rows] for i, m in enumerate(keeps)}
        for number, sequence in enumerate((bits, bits[::-1])):
            lo = number * (step // 2)
            held = {m: blocks[m][:, lo : lo + step // 2].astype(F32) for m in keeps}
            for bit in sequence:
                leaving = [m for m in held if m & bit]
                packed = jnp.stack([held[m].astype(BF) for m in leaving])
                packed = flip(packed, "fsdp", n_fsdp, bit)
                for i, m in enumerate(leaving):
                    held[m ^ bit] = held[m ^ bit] + packed[i].astype(F32)
                    del held[m]
            pieces.append(held[0])
            squares = squares + jnp.sum(held[0] * held[0])

    total = jnp.broadcast_to(squares, (8, 128))
    total = total + flip(total, "fsdp", n_fsdp, 1)
    total = total + sum(flip(total, "fsdp", n_fsdp, m) for m in keeps[1:])
    total = total + sum(
        lax.ppermute(total, "tp", [(i, (i + k) % n_tp) for i in range(n_tp)]) for k in range(1, n_tp)
    )
    mean_sq = total[0, 0] / (total_d * total_p)
    scale = lax.rsqrt(mean_sq + 1e-06)
    return jnp.concatenate([(piece * scale).astype(BF) for piece in pieces], axis=1)


def solution(mesh):
    n_fsdp, n_tp = mesh.shape["fsdp"], mesh.shape["tp"]
    placed = (P("fsdp", None), P("fsdp", None), P("fsdp"), P("fsdp", "tp"), P("fsdp", "tp"))

    def body(*args):
        return per_device(n_fsdp, n_tp, *args)

    return jax.shard_map(
        body, mesh=mesh, in_specs=placed, out_specs=P("fsdp", "tp"), check_vma=False
    )
```

```python
import functools

import jax
import jax.numpy as jnp
from jax import lax
from jax.experimental import pallas as pl
from jax.experimental.pallas import tpu as pltpu
from jax.sharding import PartitionSpec as P


LEN = 256
BF = jnp.bfloat16
F32 = jnp.float32


def dot(left, right, dims):
    return lax.dot_general(left, right, ((dims[:1], dims[1:]), ((), ())), preferred_element_type=F32)


def flip(value, axis, size, bit):
    return lax.ppermute(value, axis, [(i, i ^ bit) for i in range(size)])


def after(value, *others):
    return lax.optimization_barrier((value,) + others)[0]


def masks_of(bits):
    masks = [0]
    for bit in bits:
        masks = masks + [m | bit for m in masks]
    return sorted(masks, key=lambda m: (bin(m).count("1"), m))


def gather_near(shard, size, bits):
    return {0: shard, **{bit: flip(shard, "fsdp", size, bit) for bit in bits}}


def gather_far(got, size, bits, gate):
    got = {m: after(block, gate) for m, block in got.items()}
    half = got[0].shape[0] // 2
    low = high = None
    for mask in masks_of(bits)[1 + len(bits) :]:
        inside = [bit for bit in bits if mask & bit]
        first, last = inside[0], inside[-1]
        low, high = got[mask ^ last][:half], got[mask ^ first][half:]
        low, high = flip(low, "fsdp", size, last), flip(high, "fsdp", size, first)
        got[mask] = jnp.concatenate([low, high], axis=0)
    for mask in masks_of(bits):
        got[mask ^ 1] = flip(got[mask], "fsdp", size, 1)
    return got, (low, high)


def order_kernel(places, lengths, act_ref, cot_ref, out_ref):
    tokens = act_ref.shape[0]
    out_ref[:tokens, :] = act_ref[...]
    position = lax.broadcasted_iota(jnp.int32, (LEN, act_ref.shape[1]), 0)
    for i in range(tokens // LEN):
        rows = cot_ref[i * LEN : (i + 1) * LEN, :]
        kept = jnp.where(position < lengths[i], rows, jnp.zeros_like(rows))
        out_ref[tokens + i * LEN : tokens + (i + 1) * LEN, :] = kept


def ordered(places, lengths, activations, cotangent, cols):
    tokens, total = activations.shape
    if cols % 128:
        keep = (jnp.arange(LEN, dtype=jnp.int32)[None, :] < lengths[:, None]).reshape(-1)
        kept = jnp.where(keep[:, None], cotangent, jnp.zeros_like(cotangent))
        both = jnp.concatenate([activations, kept], axis=0)
        return jnp.concatenate(
            [lax.dynamic_slice_in_dim(both, p * cols, cols, axis=1) for p in places], axis=1
        )
    block = pl.BlockSpec((tokens, cols), lambda m, where, _: (0, where[m]))
    return pl.pallas_call(
        order_kernel,
        out_shape=jax.ShapeDtypeStruct((2 * tokens, total), activations.dtype),
        grid_spec=pltpu.PrefetchScalarGridSpec(
            num_scalar_prefetch=2,
            grid=(total // cols,),
            in_specs=[block, block],
            out_specs=pl.BlockSpec((2 * tokens, cols), lambda m, where, _: (0, m)),
        ),
        compiler_params=pltpu.CompilerParams(vmem_limit_bytes=24 << 20),
        cost_estimate=pl.CostEstimate(flops=0, bytes_accessed=8 * tokens * total, transcendentals=0),
    )(jnp.stack(places), lengths, activations, cotangent)


def scale_kernel(count, total_ref, *refs):
    refs, out_ref = refs[:-1], refs[-1]
    cols = refs[0].shape[1]
    scale = lax.rsqrt(total_ref[0:1, :] / count + 1e-06)
    scale = jnp.concatenate([scale] * (cols // 128), axis=1)
    for i, ref in enumerate(refs):
        out_ref[:, i * cols : (i + 1) * cols] = (ref[...] * scale).astype(out_ref.dtype)


def scaled(total, pieces, count):
    rows, cols = pieces[0].shape
    if cols % 128:
        scale = lax.rsqrt(total[0, 0] / count + 1e-06)
        return jnp.concatenate([(piece * scale).astype(BF) for piece in pieces], axis=1)
    return pl.pallas_call(
        functools.partial(scale_kernel, count),
        out_shape=jax.ShapeDtypeStruct((rows, cols * len(pieces)), BF),
        compiler_params=pltpu.CompilerParams(vmem_limit_bytes=16 << 20),
    )(total, *pieces)


def per_device(n_fsdp, n_tp, activations, cotangent, lengths, grow_operator, proxy_weight):
    me = lax.axis_index("fsdp")
    at = lax.axis_index("tp")
    bits = []
    while 2 << len(bits) < n_fsdp:
        bits.append(2 << len(bits))
    keeps = masks_of(bits)
    order = keeps + [m ^ 1 for m in keeps]
    tokens = activations.shape[0]
    rows, width = grow_operator.shape
    depth = proxy_weight.shape[0]
    split = len(keeps) * rows
    total_d, total_p = rows * n_fsdp, width * n_tp
    chunks = width // depth
    close = n_fsdp - 2
    last = n_tp - 1

    both = ordered([me ^ m for m in order], lengths, activations, cotangent, rows)

    w = gather_near(grow_operator, n_fsdp, bits)
    w, ends = gather_far(w, n_fsdp, bits, both)
    r = gather_near(after(proxy_weight, *ends), n_fsdp, bits)

    acc = dot(both, jnp.concatenate([w[m] for m in order], axis=0), (1, 0))
    forward = acc[:tokens].astype(BF)
    back = acc[tokens:].astype(BF)

    r, _ = gather_far(r, n_fsdp, bits, forward)

    r_near = jnp.concatenate([r[m] for m in range(close)], axis=0)
    r_far = jnp.concatenate([r[close], r[close + 1]], axis=0)
    product_near = dot(forward, r_near, (1, 1)).astype(BF)
    product_far = [dot(forward, r[close + i], (1, 1)).astype(BF) for i in range(2)]

    def place(c, owner):
        return me ^ (jnp.clip(owner, 0, last) * chunks + c)

    from_low, from_high = [back], [back]
    for hop in range(last):
        pairs = [(i, i + 1) for i in range(hop, last)]
        from_low.append(lax.ppermute(from_low[-1], "tp", pairs))
        pairs = [(last - i, last - 1 - i) for i in range(hop, last)]
        from_high.append(lax.ppermute(from_high[-1], "tp", pairs))
    back_all = jnp.zeros((tokens, total_p), BF)
    for hop in range(n_tp):
        owner = lax.rem(at - hop + n_tp, n_tp)
        for c in range(chunks):
            span = slice(c * depth, (c + 1) * depth)
            part = from_low[hop][:, span]
            if hop:
                part = part + from_high[n_tp - hop][:, span]
            back_all = lax.dynamic_update_slice_in_dim(back_all, part, place(c, owner) * depth, axis=1)
    delta = dot(back_all[:, : close * depth], r_near, (1, 0))
    delta = (delta + dot(back_all[:, close * depth :], r_far, (1, 0))).astype(BF)

    def partial(products, c, owner):
        block = place(c, owner)
        start = jnp.minimum(block, close - 1) * depth
        near = lax.dynamic_slice_in_dim(products[0], start, depth, axis=1)
        far = jnp.where(block == close, *products[1:])
        return jnp.where(block < close, near, far).astype(F32)

    products = (product_near, *product_far)
    sums, own = [], []
    for c in range(chunks):
        if c:
            products = lax.optimization_barrier(products + sums[-1][0])[:3]
        up = down = None
        hops = []
        for hop in range(1, n_tp):
            send_up, send_down = (partial(products, c, at + k) for k in (n_tp - hop, hop - n_tp))
            if up is not None:
                send_up, send_down = send_up + up, send_down + down
            send_up, send_down = send_up.astype(BF), send_down.astype(BF)
            send_up, send_down = lax.optimization_barrier((send_up, send_down))
            up = lax.ppermute(send_up, "tp", [(i, i + 1) for i in range(hop)])
            down = lax.ppermute(send_down, "tp", [(last - i, last - 1 - i) for i in range(hop)])
            hops.append((up, down))
        sums.append(hops)
        own.append(partial(products, c, at).astype(BF))

    squares = jnp.zeros((), F32)
    pieces = []
    for c in range(chunks):
        up, down = sums[c][-1]
        if c + 1 < chunks:
            up, down = after(up, *sums[c + 1][-2]), after(down, *sums[c + 1][-2])
        proxy_out = (own[c].astype(F32) + up.astype(F32) + down.astype(F32)).astype(BF)
        values = jnp.concatenate([delta[:, c * depth : (c + 1) * depth], proxy_out], axis=0)

        send = dot(both[:, split:], values, (0, 0)).astype(BF)
        arrived = flip(send, "fsdp", n_fsdp, 1)
        keep = after(dot(both[:, :split], values, (0, 0)), values)
        pair = (keep + arrived.astype(F32)).astype(BF)
        blocks = {m: pair[i * rows : (i + 1) * rows] for i, m in enumerate(keeps)}
        for number, sequence in enumerate((bits, bits[::-1])):
            lo = number * (depth // 2)
            held = {m: blocks[m][:, lo : lo + depth // 2].astype(F32) for m in keeps}
            for bit in sequence:
                leaving = [m for m in held if m & bit]
                packed = jnp.stack([held[m].astype(BF) for m in leaving])
                packed = flip(packed, "fsdp", n_fsdp, bit)
                for i, m in enumerate(leaving):
                    held[m ^ bit] = held[m ^ bit] + packed[i].astype(F32)
                    del held[m]
            pieces.append(held[0])
            squares = squares + jnp.sum(held[0] * held[0])

    total = jnp.broadcast_to(squares, (8, 128))
    total = total + flip(total, "fsdp", n_fsdp, 1)
    total = total + sum(flip(total, "fsdp", n_fsdp, m) for m in keeps[1:])
    total = total + sum(
        lax.ppermute(total, "tp", [(i, (i + k) % n_tp) for i in range(n_tp)]) for k in range(1, n_tp)
    )
    return scaled(total, pieces, total_d * total_p)


def solution(mesh):
    n_fsdp, n_tp = mesh.shape["fsdp"], mesh.shape["tp"]
    placed = (P("fsdp", None), P("fsdp", None), P("fsdp"), P("fsdp", "tp"), P("fsdp", "tp"))

    def body(*args):
        return per_device(n_fsdp, n_tp, *args)

    return jax.shard_map(
        body, mesh=mesh, in_specs=placed, out_specs=P("fsdp", "tp"), check_vma=False
    )
```

```python
import functools

import jax
import jax.numpy as jnp
from jax import lax
from jax.experimental import pallas as pl
from jax.experimental.pallas import tpu as pltpu
from jax.sharding import PartitionSpec as P


LEN = 256
BF = jnp.bfloat16
F32 = jnp.float32


def dot(left, right, dims):
    return lax.dot_general(left, right, ((dims[:1], dims[1:]), ((), ())), preferred_element_type=F32)


def flip(value, axis, size, bit):
    return lax.ppermute(value, axis, [(i, i ^ bit) for i in range(size)])


def after(value, *others):
    return lax.optimization_barrier((value,) + others)[0]


def masks_of(bits):
    masks = [0]
    for bit in bits:
        masks = masks + [m | bit for m in masks]
    return sorted(masks, key=lambda m: (bin(m).count("1"), m))


def gather_near(shard, size, bits):
    return {0: shard, **{bit: flip(shard, "fsdp", size, bit) for bit in bits}}


def gather_far(got, size, bits, gate):
    got = {m: after(block, gate) for m, block in got.items()}
    half = got[0].shape[0] // 2
    low = high = None
    for mask in masks_of(bits)[1 + len(bits) :]:
        inside = [bit for bit in bits if mask & bit]
        first, last = inside[0], inside[-1]
        low, high = got[mask ^ last][:half], got[mask ^ first][half:]
        low, high = flip(low, "fsdp", size, last), flip(high, "fsdp", size, first)
        got[mask] = jnp.concatenate([low, high], axis=0)
    for mask in masks_of(bits):
        got[mask ^ 1] = flip(got[mask], "fsdp", size, 1)
    return got, (low, high)


def order_kernel(places, lengths, act_ref, cot_ref, out_ref):
    tokens = act_ref.shape[0]
    out_ref[:tokens, :] = act_ref[...]
    position = lax.broadcasted_iota(jnp.int32, (LEN, act_ref.shape[1]), 0)
    for i in range(tokens // LEN):
        rows = cot_ref[i * LEN : (i + 1) * LEN, :]
        kept = jnp.where(position < lengths[i], rows, jnp.zeros_like(rows))
        out_ref[tokens + i * LEN : tokens + (i + 1) * LEN, :] = kept


def ordered(places, lengths, activations, cotangent, cols):
    tokens, total = activations.shape
    if cols % 128:
        keep = (jnp.arange(LEN, dtype=jnp.int32)[None, :] < lengths[:, None]).reshape(-1)
        kept = jnp.where(keep[:, None], cotangent, jnp.zeros_like(cotangent))
        both = jnp.concatenate([activations, kept], axis=0)
        return jnp.concatenate(
            [lax.dynamic_slice_in_dim(both, p * cols, cols, axis=1) for p in places], axis=1
        )
    block = pl.BlockSpec((tokens, cols), lambda m, where, _: (0, where[m]))
    return pl.pallas_call(
        order_kernel,
        out_shape=jax.ShapeDtypeStruct((2 * tokens, total), activations.dtype),
        grid_spec=pltpu.PrefetchScalarGridSpec(
            num_scalar_prefetch=2,
            grid=(total // cols,),
            in_specs=[block, block],
            out_specs=pl.BlockSpec((2 * tokens, cols), lambda m, where, _: (0, m)),
        ),
        compiler_params=pltpu.CompilerParams(vmem_limit_bytes=24 << 20),
        cost_estimate=pl.CostEstimate(flops=0, bytes_accessed=8 * tokens * total, transcendentals=0),
    )(jnp.stack(places), lengths, activations, cotangent)


def scale_kernel(count, total_ref, *refs):
    refs, out_ref = refs[:-1], refs[-1]
    cols = refs[0].shape[1]
    scale = lax.rsqrt(total_ref[0:1, :] / count + 1e-06)
    scale = jnp.concatenate([scale] * (cols // 128), axis=1)
    for i, ref in enumerate(refs):
        out_ref[:, i * cols : (i + 1) * cols] = (ref[...] * scale).astype(out_ref.dtype)


def scaled(total, pieces, count):
    rows, cols = pieces[0].shape
    if cols % 128:
        scale = lax.rsqrt(total[0, 0] / count + 1e-06)
        return jnp.concatenate([(piece * scale).astype(BF) for piece in pieces], axis=1)
    return pl.pallas_call(
        functools.partial(scale_kernel, count),
        out_shape=jax.ShapeDtypeStruct((rows, cols * len(pieces)), BF),
        compiler_params=pltpu.CompilerParams(vmem_limit_bytes=16 << 20),
    )(total, *pieces)


def unset(rows, cols):
    return pl.pallas_call(
        lambda out_ref: None,
        out_shape=jax.ShapeDtypeStruct((rows, cols), BF),
        out_specs=pl.BlockSpec(memory_space=pl.ANY),
        name="unset",
    )()


def per_device(n_fsdp, n_tp, activations, cotangent, lengths, grow_operator, proxy_weight):
    me = lax.axis_index("fsdp")
    at = lax.axis_index("tp")
    bits = []
    while 2 << len(bits) < n_fsdp:
        bits.append(2 << len(bits))
    keeps = masks_of(bits)
    order = keeps + [m ^ 1 for m in keeps]
    tokens = activations.shape[0]
    rows, width = grow_operator.shape
    depth = proxy_weight.shape[0]
    split = len(keeps) * rows
    total_d, total_p = rows * n_fsdp, width * n_tp
    chunks = width // depth
    close = n_fsdp - 2
    last = n_tp - 1
    odd = me % 2
    assert chunks == 2

    both = ordered([me ^ m for m in order], lengths, activations, cotangent, rows)

    w = gather_near(grow_operator, n_fsdp, bits)
    w, ends = gather_far(w, n_fsdp, bits, both)
    r = gather_near(after(proxy_weight, *ends), n_fsdp, bits)

    acc = dot(both, jnp.concatenate([w[m] for m in order], axis=0), (1, 0))
    forward = acc[:tokens].astype(BF)
    back = acc[tokens:].astype(BF)

    r, _ = gather_far(r, n_fsdp, bits, forward)

    r_all = unset(total_p, width)
    for m in range(close):
        r_all = lax.dynamic_update_slice_in_dim(r_all, r[m], (m ^ odd) * depth, axis=0)
    product_near = dot(forward, r_all[: close * depth], (1, 1)).astype(BF)
    for m in range(close, n_fsdp):
        block = after(r[m], product_near)
        r_all = lax.dynamic_update_slice_in_dim(r_all, block, (m ^ odd) * depth, axis=0)
    product_far = [dot(forward, r[close + i], (1, 1)).astype(BF) for i in range(2)]

    def place(c, owner):
        return me ^ (jnp.clip(owner, 0, last) * chunks + c)

    from_low, from_high = [back], [back]
    for hop in range(last):
        pairs = [(i, i + 1) for i in range(hop, last)]
        from_low.append(lax.ppermute(from_low[-1], "tp", pairs))
        pairs = [(last - i, last - 1 - i) for i in range(hop, last)]
        from_high.append(lax.ppermute(from_high[-1], "tp", pairs))
    back_all = unset(tokens, total_p)
    for hop in range(n_tp):
        owner = lax.rem(at - hop + n_tp, n_tp)
        column = (me // 2 ^ owner) * width
        if hop:
            piece = from_low[hop] + from_high[n_tp - hop]
            back_all = lax.dynamic_update_slice_in_dim(back_all, piece, column, axis=1)
        else:
            for c in range(chunks):
                piece = back[:, c * depth : (c + 1) * depth]
                back_all = lax.dynamic_update_slice_in_dim(back_all, piece, column + c * depth, axis=1)
    delta = dot(back_all, r_all, (1, 0)).astype(BF)

    def partial(products, c, owner):
        block = place(c, owner)
        start = (jnp.minimum(block, close - 1) ^ odd) * depth
        near = lax.dynamic_slice_in_dim(products[0], start, depth, axis=1)
        far = jnp.where(block == close, *products[1:])
        return jnp.where(block < close, near, far).astype(F32)

    products = (product_near, *product_far)
    sums, own = [], []
    for c in range(chunks):
        if c:
            products = lax.optimization_barrier(products + sums[-1][min(1, last - 1)])[:3]
        up = down = None
        hops = []
        for hop in range(1, n_tp):
            send_up, send_down = (partial(products, c, at + k) for k in (n_tp - hop, hop - n_tp))
            if up is not None:
                send_up, send_down = send_up + up, send_down + down
            send_up, send_down = send_up.astype(BF), send_down.astype(BF)
            send_up, send_down = lax.optimization_barrier((send_up, send_down))
            up = lax.ppermute(send_up, "tp", [(i, i + 1) for i in range(hop)])
            down = lax.ppermute(send_down, "tp", [(last - i, last - 1 - i) for i in range(hop)])
            hops.append((up, down))
        sums.append(hops)
        own.append(partial(products, c, at).astype(BF))

    squares = jnp.zeros((), F32)
    pieces = []
    for c in range(chunks):
        up, down = sums[c][-1]
        if c + 1 < chunks:
            up, down = after(up, *sums[c + 1][-3]), after(down, *sums[c + 1][-3])
        proxy_out = (own[c].astype(F32) + up.astype(F32) + down.astype(F32)).astype(BF)
        values = jnp.concatenate([delta[:, c * depth : (c + 1) * depth], proxy_out], axis=0)

        send = dot(both[:, split:], values, (0, 0)).astype(BF)
        arrived = flip(send, "fsdp", n_fsdp, 1)
        keep = after(dot(both[:, :split], values, (0, 0)), values)
        pair = (keep + arrived.astype(F32)).astype(BF)
        blocks = {m: pair[i * rows : (i + 1) * rows] for i, m in enumerate(keeps)}
        half = depth // 2
        halves = [
            {m: blocks[m][:, n * half : (n + 1) * half].astype(F32) for m in keeps} for n in range(2)
        ]
        for turn in range(len(bits)):
            arrived = []
            for held, bit in zip(halves, (bits[turn], bits[-1 - turn])):
                packed = jnp.stack([held[m].astype(BF) for m in held if m & bit])
                arrived.append(flip(packed, "fsdp", n_fsdp, bit))
            arrived = lax.optimization_barrier(tuple(arrived))
            for held, bit, packed in zip(halves, (bits[turn], bits[-1 - turn]), arrived):
                for i, m in enumerate([m for m in held if m & bit]):
                    held[m ^ bit] = held[m ^ bit] + packed[i].astype(F32)
                    del held[m]
        for held in halves:
            pieces.append(held[0])
            squares = squares + jnp.sum(held[0] * held[0])

    total = jnp.broadcast_to(squares, (8, 128))
    total = total + flip(total, "fsdp", n_fsdp, 1)
    total = total + sum(flip(total, "fsdp", n_fsdp, m) for m in keeps[1:])
    total = total + sum(
        lax.ppermute(total, "tp", [(i, (i + k) % n_tp) for i in range(n_tp)]) for k in range(1, n_tp)
    )
    return scaled(total, pieces, total_d * total_p)


def solution(mesh):
    n_fsdp, n_tp = mesh.shape["fsdp"], mesh.shape["tp"]
    placed = (P("fsdp", None), P("fsdp", None), P("fsdp"), P("fsdp", "tp"), P("fsdp", "tp"))

    def body(*args):
        return per_device(n_fsdp, n_tp, *args)

    return jax.shard_map(
        body, mesh=mesh, in_specs=placed, out_specs=P("fsdp", "tp"), check_vma=False
    )
```

```python
import functools

import jax
import jax.numpy as jnp
from jax import lax
from jax.experimental import pallas as pl
from jax.experimental.pallas import tpu as pltpu
from jax.sharding import PartitionSpec as P


LEN = 256
BF = jnp.bfloat16
F32 = jnp.float32


def dot(left, right, dims):
    return lax.dot_general(left, right, ((dims[:1], dims[1:]), ((), ())), preferred_element_type=F32)


def flip(value, axis, size, bit):
    return lax.ppermute(value, axis, [(i, i ^ bit) for i in range(size)])


def after(value, *others):
    return lax.optimization_barrier((value,) + others)[0]


def masks_of(bits):
    masks = [0]
    for bit in bits:
        masks = masks + [m | bit for m in masks]
    return sorted(masks, key=lambda m: (bin(m).count("1"), m))


def gather_near(shard, size, bits):
    return {0: shard, **{bit: flip(shard, "fsdp", size, bit) for bit in bits}}


def gather_far(got, size, bits, gate):
    got = {m: after(block, gate) for m, block in got.items()}
    half = got[0].shape[0] // 2
    low = high = None
    for mask in masks_of(bits)[1 + len(bits) :]:
        inside = [bit for bit in bits if mask & bit]
        first, last = inside[0], inside[-1]
        low, high = got[mask ^ last][:half], got[mask ^ first][half:]
        low, high = flip(low, "fsdp", size, last), flip(high, "fsdp", size, first)
        got[mask] = jnp.concatenate([low, high], axis=0)
    for mask in masks_of(bits):
        got[mask ^ 1] = flip(got[mask], "fsdp", size, 1)
    return got, (low, high)


def order_kernel(places, lengths, act_ref, cot_ref, out_ref):
    tokens = act_ref.shape[0]
    out_ref[:tokens, :] = act_ref[...]
    position = lax.broadcasted_iota(jnp.int32, (LEN, act_ref.shape[1]), 0)
    for i in range(tokens // LEN):
        rows = cot_ref[i * LEN : (i + 1) * LEN, :]
        kept = jnp.where(position < lengths[i], rows, jnp.zeros_like(rows))
        out_ref[tokens + i * LEN : tokens + (i + 1) * LEN, :] = kept


def ordered(places, lengths, activations, cotangent, cols):
    tokens, total = activations.shape
    if cols % 128:
        keep = (jnp.arange(LEN, dtype=jnp.int32)[None, :] < lengths[:, None]).reshape(-1)
        kept = jnp.where(keep[:, None], cotangent, jnp.zeros_like(cotangent))
        both = jnp.concatenate([activations, kept], axis=0)
        return jnp.concatenate(
            [lax.dynamic_slice_in_dim(both, p * cols, cols, axis=1) for p in places], axis=1
        )
    block = pl.BlockSpec((tokens, cols), lambda m, where, _: (0, where[m]))
    return pl.pallas_call(
        order_kernel,
        out_shape=jax.ShapeDtypeStruct((2 * tokens, total), activations.dtype),
        grid_spec=pltpu.PrefetchScalarGridSpec(
            num_scalar_prefetch=2,
            grid=(total // cols,),
            in_specs=[block, block],
            out_specs=pl.BlockSpec((2 * tokens, cols), lambda m, where, _: (0, m)),
        ),
        compiler_params=pltpu.CompilerParams(vmem_limit_bytes=24 << 20),
        cost_estimate=pl.CostEstimate(flops=0, bytes_accessed=8 * tokens * total, transcendentals=0),
    )(jnp.stack(places), lengths, activations, cotangent)


def scale_kernel(count, total_ref, *refs):
    refs, out_ref = refs[:-1], refs[-1]
    cols = refs[0].shape[1]
    scale = lax.rsqrt(total_ref[0:1, :] / count + 1e-06)
    scale = jnp.concatenate([scale] * (cols // 128), axis=1)
    for i, ref in enumerate(refs):
        out_ref[:, i * cols : (i + 1) * cols] = (ref[...] * scale).astype(out_ref.dtype)


def scaled(total, pieces, count):
    rows, cols = pieces[0].shape
    if cols % 128:
        scale = lax.rsqrt(total[0, 0] / count + 1e-06)
        return jnp.concatenate([(piece * scale).astype(BF) for piece in pieces], axis=1)
    return pl.pallas_call(
        functools.partial(scale_kernel, count),
        out_shape=jax.ShapeDtypeStruct((rows, cols * len(pieces)), BF),
        compiler_params=pltpu.CompilerParams(vmem_limit_bytes=16 << 20),
    )(total, *pieces)


def per_device(n_fsdp, n_tp, activations, cotangent, lengths, grow_operator, proxy_weight):
    me = lax.axis_index("fsdp")
    at = lax.axis_index("tp")
    bits = []
    while 2 << len(bits) < n_fsdp:
        bits.append(2 << len(bits))
    keeps = masks_of(bits)
    order = keeps + [m ^ 1 for m in keeps]
    tokens = activations.shape[0]
    rows, width = grow_operator.shape
    depth = proxy_weight.shape[0]
    split = len(keeps) * rows
    total_d, total_p = rows * n_fsdp, width * n_tp
    chunks = width // depth
    close = n_fsdp - 2
    last = n_tp - 1

    both = ordered([me ^ m for m in order], lengths, activations, cotangent, rows)

    w = gather_near(grow_operator, n_fsdp, bits)
    w, ends = gather_far(w, n_fsdp, bits, both)
    r = gather_near(after(proxy_weight, *ends), n_fsdp, bits)

    acc = dot(both, jnp.concatenate([w[m] for m in order], axis=0), (1, 0))
    forward = acc[:tokens].astype(BF)
    back = acc[tokens:].astype(BF)

    r, _ = gather_far(r, n_fsdp, bits, forward)

    r_near = jnp.concatenate([r[m] for m in range(close)], axis=0)
    r_far = jnp.concatenate([r[close], r[close + 1]], axis=0)
    product_near = dot(forward, r_near, (1, 1)).astype(BF)
    product_far = [dot(forward, r[close + i], (1, 1)).astype(BF) for i in range(2)]

    def place(c, owner):
        return me ^ (jnp.clip(owner, 0, last) * chunks + c)

    from_low, from_high = [back], [back]
    for hop in range(last):
        pairs = [(i, i + 1) for i in range(hop, last)]
        from_low.append(lax.ppermute(from_low[-1], "tp", pairs))
        pairs = [(last - i, last - 1 - i) for i in range(hop, last)]
        from_high.append(lax.ppermute(from_high[-1], "tp", pairs))
    back_all = jnp.zeros((tokens, total_p), BF)
    for hop in range(n_tp):
        owner = lax.rem(at - hop + n_tp, n_tp)
        for c in range(chunks):
            span = slice(c * depth, (c + 1) * depth)
            part = from_low[hop][:, span]
            if hop:
                part = part + from_high[n_tp - hop][:, span]
            back_all = lax.dynamic_update_slice_in_dim(back_all, part, place(c, owner) * depth, axis=1)
    delta = dot(back_all[:, : close * depth], r_near, (1, 0))
    delta = (delta + dot(back_all[:, close * depth :], r_far, (1, 0))).astype(BF)

    def partial(products, c, owner):
        block = place(c, owner)
        start = jnp.minimum(block, close - 1) * depth
        near = lax.dynamic_slice_in_dim(products[0], start, depth, axis=1)
        far = jnp.where(block == close, *products[1:])
        return jnp.where(block < close, near, far).astype(F32)

    products = (product_near, *product_far)
    sums, own = [], []
    for c in range(chunks):
        if c:
            products = lax.optimization_barrier(products + sums[-1][0])[:3]
        up = down = None
        hops = []
        for hop in range(1, n_tp):
            send_up, send_down = (partial(products, c, at + k) for k in (n_tp - hop, hop - n_tp))
            if up is not None:
                send_up, send_down = send_up + up, send_down + down
            send_up, send_down = send_up.astype(BF), send_down.astype(BF)
            send_up, send_down = lax.optimization_barrier((send_up, send_down))
            up = lax.ppermute(send_up, "tp", [(i, i + 1) for i in range(hop)])
            down = lax.ppermute(send_down, "tp", [(last - i, last - 1 - i) for i in range(hop)])
            hops.append((up, down))
        sums.append(hops)
        own.append(partial(products, c, at).astype(BF))

    squares = jnp.zeros((), F32)
    pieces = []
    for c in range(chunks):
        up, down = sums[c][-1]
        if c + 1 < chunks:
            up, down = after(up, *sums[c + 1][-2]), after(down, *sums[c + 1][-2])
        proxy_out = (own[c].astype(F32) + up.astype(F32) + down.astype(F32)).astype(BF)
        values = jnp.concatenate([delta[:, c * depth : (c + 1) * depth], proxy_out], axis=0)

        send = dot(both[:, split:], values, (0, 0)).astype(BF)
        arrived = flip(send, "fsdp", n_fsdp, 1)
        keep = after(dot(both[:, :split], values, (0, 0)), values)
        pair = (keep + arrived.astype(F32)).astype(BF)
        blocks = {m: pair[i * rows : (i + 1) * rows] for i, m in enumerate(keeps)}
        half = depth // 2
        halves = [
            {m: blocks[m][:, n * half : (n + 1) * half].astype(F32) for m in keeps} for n in range(2)
        ]
        for turn in range(len(bits)):
            arrived = []
            for held, bit in zip(halves, (bits[turn], bits[-1 - turn])):
                packed = jnp.stack([held[m].astype(BF) for m in held if m & bit])
                arrived.append(flip(packed, "fsdp", n_fsdp, bit))
            arrived = lax.optimization_barrier(tuple(arrived))
            for held, bit, packed in zip(halves, (bits[turn], bits[-1 - turn]), arrived):
                for i, m in enumerate([m for m in held if m & bit]):
                    held[m ^ bit] = held[m ^ bit] + packed[i].astype(F32)
                    del held[m]
        for held in halves:
            pieces.append(held[0])
            squares = squares + jnp.sum(held[0] * held[0])

    total = jnp.broadcast_to(squares, (8, 128))
    total = total + flip(total, "fsdp", n_fsdp, 1)
    total = total + sum(flip(total, "fsdp", n_fsdp, m) for m in keeps[1:])
    total = total + sum(
        lax.ppermute(total, "tp", [(i, (i + k) % n_tp) for i in range(n_tp)]) for k in range(1, n_tp)
    )
    return scaled(total, pieces, total_d * total_p)


def solution(mesh):
    n_fsdp, n_tp = mesh.shape["fsdp"], mesh.shape["tp"]
    placed = (P("fsdp", None), P("fsdp", None), P("fsdp"), P("fsdp", "tp"), P("fsdp", "tp"))

    def body(*args):
        return per_device(n_fsdp, n_tp, *args)

    return jax.shard_map(
        body, mesh=mesh, in_specs=placed, out_specs=P("fsdp", "tp"), check_vma=False
    )
```

```python
import functools

import jax
import jax.numpy as jnp
from jax import lax
from jax.experimental import pallas as pl
from jax.experimental.pallas import tpu as pltpu
from jax.sharding import PartitionSpec as P


LEN = 256
BF = jnp.bfloat16
F32 = jnp.float32


def dot(left, right, dims):
    return lax.dot_general(left, right, ((dims[:1], dims[1:]), ((), ())), preferred_element_type=F32)


def flip(value, axis, size, bit):
    return lax.ppermute(value, axis, [(i, i ^ bit) for i in range(size)])


def after(value, *others):
    return lax.optimization_barrier((value,) + others)[0]


def masks_of(bits):
    masks = [0]
    for bit in bits:
        masks = masks + [m | bit for m in masks]
    return sorted(masks, key=lambda m: (bin(m).count("1"), m))


def gather_near(shard, size, bits):
    return {0: shard, **{bit: flip(shard, "fsdp", size, bit) for bit in bits}}


def gather_far(got, size, bits, gate):
    got = {m: after(block, gate) for m, block in got.items()}
    half = got[0].shape[0] // 2
    low = high = None
    for mask in masks_of(bits)[1 + len(bits) :]:
        inside = [bit for bit in bits if mask & bit]
        first, last = inside[0], inside[-1]
        low, high = got[mask ^ last][:half], got[mask ^ first][half:]
        low, high = flip(low, "fsdp", size, last), flip(high, "fsdp", size, first)
        got[mask] = jnp.concatenate([low, high], axis=0)
    for mask in masks_of(bits):
        got[mask ^ 1] = flip(got[mask], "fsdp", size, 1)
    return got, (low, high)


def order_kernel(places, lengths, act_ref, cot_ref, out_ref):
    tokens = act_ref.shape[0]
    out_ref[:tokens, :] = act_ref[...]
    position = lax.broadcasted_iota(jnp.int32, (LEN, act_ref.shape[1]), 0)
    for i in range(tokens // LEN):
        rows = cot_ref[i * LEN : (i + 1) * LEN, :]
        kept = jnp.where(position < lengths[i], rows, jnp.zeros_like(rows))
        out_ref[tokens + i * LEN : tokens + (i + 1) * LEN, :] = kept


def ordered(places, lengths, activations, cotangent, cols):
    tokens, total = activations.shape
    if cols % 128:
        keep = (jnp.arange(LEN, dtype=jnp.int32)[None, :] < lengths[:, None]).reshape(-1)
        kept = jnp.where(keep[:, None], cotangent, jnp.zeros_like(cotangent))
        both = jnp.concatenate([activations, kept], axis=0)
        return jnp.concatenate(
            [lax.dynamic_slice_in_dim(both, p * cols, cols, axis=1) for p in places], axis=1
        )
    block = pl.BlockSpec((tokens, cols), lambda m, where, _: (0, where[m]))
    return pl.pallas_call(
        order_kernel,
        out_shape=jax.ShapeDtypeStruct((2 * tokens, total), activations.dtype),
        grid_spec=pltpu.PrefetchScalarGridSpec(
            num_scalar_prefetch=2,
            grid=(total // cols,),
            in_specs=[block, block],
            out_specs=pl.BlockSpec((2 * tokens, cols), lambda m, where, _: (0, m)),
        ),
        compiler_params=pltpu.CompilerParams(vmem_limit_bytes=24 << 20),
        cost_estimate=pl.CostEstimate(flops=0, bytes_accessed=8 * tokens * total, transcendentals=0),
    )(jnp.stack(places), lengths, activations, cotangent)


def scale_kernel(count, total_ref, *refs):
    refs, out_ref = refs[:-1], refs[-1]
    cols = refs[0].shape[1]
    scale = lax.rsqrt(total_ref[0:1, :] / count + 1e-06)
    scale = jnp.concatenate([scale] * (cols // 128), axis=1)
    for i, ref in enumerate(refs):
        out_ref[:, i * cols : (i + 1) * cols] = (ref[...] * scale).astype(out_ref.dtype)


def scaled(total, pieces, count):
    rows, cols = pieces[0].shape
    if cols % 128:
        scale = lax.rsqrt(total[0, 0] / count + 1e-06)
        return jnp.concatenate([(piece * scale).astype(BF) for piece in pieces], axis=1)
    return pl.pallas_call(
        functools.partial(scale_kernel, count),
        out_shape=jax.ShapeDtypeStruct((rows, cols * len(pieces)), BF),
        compiler_params=pltpu.CompilerParams(vmem_limit_bytes=16 << 20),
    )(total, *pieces)


def per_device(n_fsdp, n_tp, activations, cotangent, lengths, grow_operator, proxy_weight):
    me = lax.axis_index("fsdp")
    at = lax.axis_index("tp")
    bits = []
    while 2 << len(bits) < n_fsdp:
        bits.append(2 << len(bits))
    keeps = masks_of(bits)
    order = keeps + [m ^ 1 for m in keeps]
    tokens = activations.shape[0]
    rows, width = grow_operator.shape
    depth = proxy_weight.shape[0]
    split = len(keeps) * rows
    total_d, total_p = rows * n_fsdp, width * n_tp
    chunks = width // depth
    close = n_fsdp - 2
    last = n_tp - 1

    both = ordered([me ^ m for m in order], lengths, activations, cotangent, rows)

    w = gather_near(grow_operator, n_fsdp, bits)
    w, ends = gather_far(w, n_fsdp, bits, both)
    r = gather_near(after(proxy_weight, *ends), n_fsdp, bits)

    acc = dot(both, jnp.concatenate([w[m] for m in order], axis=0), (1, 0))
    forward = acc[:tokens].astype(BF)
    back = acc[tokens:].astype(BF)

    r, _ = gather_far(r, n_fsdp, bits, forward)

    assert chunks == 2
    odd = me % 2
    r_all = jnp.zeros((total_p, width), BF)
    for m in range(close):
        r_all = lax.dynamic_update_slice_in_dim(r_all, r[m], (m ^ odd) * depth, axis=0)
    product_near = dot(forward, r_all[: close * depth], (1, 1)).astype(BF)
    for m in range(close, n_fsdp):
        block = after(r[m], product_near)
        r_all = lax.dynamic_update_slice_in_dim(r_all, block, (m ^ odd) * depth, axis=0)
    product_far = [dot(forward, r[close + i], (1, 1)).astype(BF) for i in range(2)]

    def place(c, owner):
        return me ^ (jnp.clip(owner, 0, last) * chunks + c)

    from_low, from_high = [back], [back]
    for hop in range(last):
        pairs = [(i, i + 1) for i in range(hop, last)]
        from_low.append(lax.ppermute(from_low[-1], "tp", pairs))
        pairs = [(last - i, last - 1 - i) for i in range(hop, last)]
        from_high.append(lax.ppermute(from_high[-1], "tp", pairs))
    delta = None
    for hop in sorted(range(n_tp), key=lambda hop: max(hop, n_tp - hop) if hop else 0):
        piece = from_low[hop] + from_high[n_tp - hop] if hop else back
        owner = lax.rem(at - hop + n_tp, n_tp)
        block = lax.dynamic_slice_in_dim(r_all, (me // 2 ^ owner) * width, width, axis=0)
        part = dot(piece, block, (1, 0))
        delta = part if delta is None else delta + part
    delta = delta.astype(BF)

    def partial(products, c, owner):
        block = place(c, owner)
        start = (jnp.minimum(block, close - 1) ^ odd) * depth
        near = lax.dynamic_slice_in_dim(products[0], start, depth, axis=1)
        far = jnp.where(block == close, *products[1:])
        return jnp.where(block < close, near, far).astype(F32)

    products = (product_near, *product_far)
    sums, own = [], []
    for c in range(chunks):
        if c:
            products = lax.optimization_barrier(products + sums[-1][0])[:3]
        up = down = None
        hops = []
        for hop in range(1, n_tp):
            send_up, send_down = (partial(products, c, at + k) for k in (n_tp - hop, hop - n_tp))
            if up is not None:
                send_up, send_down = send_up + up, send_down + down
            send_up, send_down = send_up.astype(BF), send_down.astype(BF)
            send_up, send_down = lax.optimization_barrier((send_up, send_down))
            up = lax.ppermute(send_up, "tp", [(i, i + 1) for i in range(hop)])
            down = lax.ppermute(send_down, "tp", [(last - i, last - 1 - i) for i in range(hop)])
            hops.append((up, down))
        sums.append(hops)
        own.append(partial(products, c, at).astype(BF))

    squares = jnp.zeros((), F32)
    pieces = []
    for c in range(chunks):
        up, down = sums[c][-1]
        if c + 1 < chunks:
            up, down = after(up, *sums[c + 1][-2]), after(down, *sums[c + 1][-2])
        proxy_out = (own[c].astype(F32) + up.astype(F32) + down.astype(F32)).astype(BF)
        values = jnp.concatenate([delta[:, c * depth : (c + 1) * depth], proxy_out], axis=0)

        send = dot(both[:, split:], values, (0, 0)).astype(BF)
        arrived = flip(send, "fsdp", n_fsdp, 1)
        keep = after(dot(both[:, :split], values, (0, 0)).astype(BF), values)
        pair = (keep.astype(F32) + arrived.astype(F32)).astype(BF)
        blocks = {m: pair[i * rows : (i + 1) * rows] for i, m in enumerate(keeps)}
        half = depth // 2
        halves = [
            {m: blocks[m][:, n * half : (n + 1) * half].astype(F32) for m in keeps} for n in range(2)
        ]
        for turn in range(len(bits)):
            arrived = []
            for held, bit in zip(halves, (bits[turn], bits[-1 - turn])):
                packed = jnp.stack([held[m].astype(BF) for m in held if m & bit])
                arrived.append(flip(packed, "fsdp", n_fsdp, bit))
            arrived = lax.optimization_barrier(tuple(arrived))
            for held, bit, packed in zip(halves, (bits[turn], bits[-1 - turn]), arrived):
                for i, m in enumerate([m for m in held if m & bit]):
                    held[m ^ bit] = held[m ^ bit] + packed[i].astype(F32)
                    del held[m]
        for held in halves:
            pieces.append(held[0])
            squares = squares + jnp.sum(held[0] * held[0])

    total = jnp.broadcast_to(squares, (8, 128))
    total = total + flip(total, "fsdp", n_fsdp, 1)
    total = total + sum(flip(total, "fsdp", n_fsdp, m) for m in keeps[1:])
    total = total + sum(
        lax.ppermute(total, "tp", [(i, (i + k) % n_tp) for i in range(n_tp)]) for k in range(1, n_tp)
    )
    return scaled(total, pieces, total_d * total_p)


def solution(mesh):
    n_fsdp, n_tp = mesh.shape["fsdp"], mesh.shape["tp"]
    placed = (P("fsdp", None), P("fsdp", None), P("fsdp"), P("fsdp", "tp"), P("fsdp", "tp"))

    def body(*args):
        return per_device(n_fsdp, n_tp, *args)

    return jax.shard_map(
        body, mesh=mesh, in_specs=placed, out_specs=P("fsdp", "tp"), check_vma=False
    )
```

```python
import functools

import jax
import jax.numpy as jnp
from jax import lax
from jax.experimental import pallas as pl
from jax.experimental.pallas import tpu as pltpu
from jax.sharding import PartitionSpec as P


LEN = 256
BF = jnp.bfloat16
F32 = jnp.float32


def dot(left, right, dims):
    return lax.dot_general(left, right, ((dims[:1], dims[1:]), ((), ())), preferred_element_type=F32)


def flip(value, axis, size, bit):
    return lax.ppermute(value, axis, [(i, i ^ bit) for i in range(size)])


def after(value, *others):
    return lax.optimization_barrier((value,) + others)[0]


def masks_of(bits):
    masks = [0]
    for bit in bits:
        masks = masks + [m | bit for m in masks]
    return sorted(masks, key=lambda m: (bin(m).count("1"), m))


def gather_near(shard, size, bits):
    return {0: shard, **{bit: flip(shard, "fsdp", size, bit) for bit in bits}}


def gather_far(got, size, bits, gate):
    got = {m: after(block, gate) for m, block in got.items()}
    half = got[0].shape[0] // 2
    low = high = None
    for mask in masks_of(bits)[1 + len(bits) :]:
        inside = [bit for bit in bits if mask & bit]
        first, last = inside[0], inside[-1]
        low, high = got[mask ^ last][:half], got[mask ^ first][half:]
        low, high = flip(low, "fsdp", size, last), flip(high, "fsdp", size, first)
        got[mask] = jnp.concatenate([low, high], axis=0)
    for mask in masks_of(bits):
        got[mask ^ 1] = flip(got[mask], "fsdp", size, 1)
    return got, (low, high)


def order_kernel(places, lengths, act_ref, cot_ref, out_ref):
    tokens = act_ref.shape[0]
    out_ref[:tokens, :] = act_ref[...]
    position = lax.broadcasted_iota(jnp.int32, (LEN, act_ref.shape[1]), 0)
    for i in range(tokens // LEN):
        rows = cot_ref[i * LEN : (i + 1) * LEN, :]
        kept = jnp.where(position < lengths[i], rows, jnp.zeros_like(rows))
        out_ref[tokens + i * LEN : tokens + (i + 1) * LEN, :] = kept


def ordered(places, lengths, activations, cotangent, cols):
    tokens, total = activations.shape
    if cols % 128:
        keep = (jnp.arange(LEN, dtype=jnp.int32)[None, :] < lengths[:, None]).reshape(-1)
        kept = jnp.where(keep[:, None], cotangent, jnp.zeros_like(cotangent))
        both = jnp.concatenate([activations, kept], axis=0)
        return jnp.concatenate(
            [lax.dynamic_slice_in_dim(both, p * cols, cols, axis=1) for p in places], axis=1
        )
    block = pl.BlockSpec((tokens, cols), lambda m, where, _: (0, where[m]))
    return pl.pallas_call(
        order_kernel,
        out_shape=jax.ShapeDtypeStruct((2 * tokens, total), activations.dtype),
        grid_spec=pltpu.PrefetchScalarGridSpec(
            num_scalar_prefetch=2,
            grid=(total // cols,),
            in_specs=[block, block],
            out_specs=pl.BlockSpec((2 * tokens, cols), lambda m, where, _: (0, m)),
        ),
        compiler_params=pltpu.CompilerParams(vmem_limit_bytes=24 << 20),
        cost_estimate=pl.CostEstimate(flops=0, bytes_accessed=8 * tokens * total, transcendentals=0),
    )(jnp.stack(places), lengths, activations, cotangent)


def scale_kernel(count, total_ref, *refs):
    refs, out_ref = refs[:-1], refs[-1]
    cols = refs[0].shape[1]
    scale = lax.rsqrt(total_ref[0:1, :] / count + 1e-06)
    scale = jnp.concatenate([scale] * (cols // 128), axis=1)
    for i, ref in enumerate(refs):
        out_ref[:, i * cols : (i + 1) * cols] = (ref[...] * scale).astype(out_ref.dtype)


def scaled(total, pieces, count):
    rows, cols = pieces[0].shape
    if cols % 128:
        scale = lax.rsqrt(total[0, 0] / count + 1e-06)
        return jnp.concatenate([(piece * scale).astype(BF) for piece in pieces], axis=1)
    return pl.pallas_call(
        functools.partial(scale_kernel, count),
        out_shape=jax.ShapeDtypeStruct((rows, cols * len(pieces)), BF),
        compiler_params=pltpu.CompilerParams(vmem_limit_bytes=16 << 20),
    )(total, *pieces)


def unset(rows, cols):
    return pl.pallas_call(
        lambda out_ref: None,
        out_shape=jax.ShapeDtypeStruct((rows, cols), BF),
        out_specs=pl.BlockSpec(memory_space=pl.ANY),
        name="unset",
    )()


def per_device(n_fsdp, n_tp, activations, cotangent, lengths, grow_operator, proxy_weight):
    me = lax.axis_index("fsdp")
    at = lax.axis_index("tp")
    bits = []
    while 2 << len(bits) < n_fsdp:
        bits.append(2 << len(bits))
    keeps = masks_of(bits)
    order = keeps + [m ^ 1 for m in keeps]
    tokens = activations.shape[0]
    rows, width = grow_operator.shape
    depth = proxy_weight.shape[0]
    split = len(keeps) * rows
    total_d, total_p = rows * n_fsdp, width * n_tp
    chunks = width // depth
    close = n_fsdp - 2
    last = n_tp - 1

    both = ordered([me ^ m for m in order], lengths, activations, cotangent, rows)

    w = gather_near(grow_operator, n_fsdp, bits)
    w, ends = gather_far(w, n_fsdp, bits, both)
    r = gather_near(after(proxy_weight, *ends), n_fsdp, bits)

    acc = dot(both, jnp.concatenate([w[m] for m in order], axis=0), (1, 0))
    forward = acc[:tokens].astype(BF)
    back = acc[tokens:].astype(BF)

    r, _ = gather_far(r, n_fsdp, bits, forward)

    assert chunks == 2
    odd = me % 2
    r_near = jnp.concatenate([r[m] for m in range(close)], axis=0)
    product_near = dot(forward, r_near, (1, 1)).astype(BF)
    product_far = [dot(forward, r[close + i], (1, 1)).astype(BF) for i in range(2)]
    r_all = unset(total_p, width)
    for m in range(n_fsdp):
        block = after(r[m], product_far[0])
        r_all = lax.dynamic_update_slice_in_dim(r_all, block, (m ^ odd) * depth, axis=0)

    def place(c, owner):
        return me ^ (jnp.clip(owner, 0, last) * chunks + c)

    from_low, from_high = [back], [back]
    for hop in range(last):
        pairs = [(i, i + 1) for i in range(hop, last)]
        from_low.append(lax.ppermute(from_low[-1], "tp", pairs))
        pairs = [(last - i, last - 1 - i) for i in range(hop, last)]
        from_high.append(lax.ppermute(from_high[-1], "tp", pairs))
    delta = None
    for hop in sorted(range(n_tp), key=lambda hop: max(hop, n_tp - hop) if hop else 0):
        piece = from_low[hop] + from_high[n_tp - hop] if hop else back
        owner = lax.rem(at - hop + n_tp, n_tp)
        block = lax.dynamic_slice_in_dim(r_all, (me // 2 ^ owner) * width, width, axis=0)
        part = dot(piece, block, (1, 0))
        delta = part if delta is None else delta + part
    delta = delta.astype(BF)

    def partial(products, c, owner):
        block = place(c, owner)
        start = jnp.minimum(block, close - 1) * depth
        near = lax.dynamic_slice_in_dim(products[0], start, depth, axis=1)
        far = jnp.where(block == close, *products[1:])
        return jnp.where(block < close, near, far).astype(F32)

    products = (product_near, *product_far)
    sums, own = [], []
    for c in range(chunks):
        if c:
            products = lax.optimization_barrier(products + sums[-1][0])[:3]
        up = down = None
        hops = []
        for hop in range(1, n_tp):
            send_up, send_down = (partial(products, c, at + k) for k in (n_tp - hop, hop - n_tp))
            if up is not None:
                send_up, send_down = send_up + up, send_down + down
            send_up, send_down = send_up.astype(BF), send_down.astype(BF)
            send_up, send_down = lax.optimization_barrier((send_up, send_down))
            up = lax.ppermute(send_up, "tp", [(i, i + 1) for i in range(hop)])
            down = lax.ppermute(send_down, "tp", [(last - i, last - 1 - i) for i in range(hop)])
            hops.append((up, down))
        sums.append(hops)
        own.append(partial(products, c, at).astype(BF))

    squares = jnp.zeros((), F32)
    pieces = []
    for c in range(chunks):
        up, down = sums[c][-1]
        if c + 1 < chunks:
            up, down = after(up, *sums[c + 1][-2]), after(down, *sums[c + 1][-2])
        proxy_out = (own[c].astype(F32) + up.astype(F32) + down.astype(F32)).astype(BF)
        values = jnp.concatenate([delta[:, c * depth : (c + 1) * depth], proxy_out], axis=0)

        send = dot(both[:, split:], values, (0, 0)).astype(BF)
        arrived = flip(send, "fsdp", n_fsdp, 1)
        keep = after(dot(both[:, :split], values, (0, 0)).astype(BF), values)
        pair = (keep.astype(F32) + arrived.astype(F32)).astype(BF)
        blocks = {m: pair[i * rows : (i + 1) * rows] for i, m in enumerate(keeps)}
        half = depth // 2
        halves = [
            {m: blocks[m][:, n * half : (n + 1) * half].astype(F32) for m in keeps} for n in range(2)
        ]
        for turn in range(len(bits)):
            arrived = []
            for held, bit in zip(halves, (bits[turn], bits[-1 - turn])):
                packed = jnp.stack([held[m].astype(BF) for m in held if m & bit])
                arrived.append(flip(packed, "fsdp", n_fsdp, bit))
            arrived = lax.optimization_barrier(tuple(arrived))
            for held, bit, packed in zip(halves, (bits[turn], bits[-1 - turn]), arrived):
                for i, m in enumerate([m for m in held if m & bit]):
                    held[m ^ bit] = held[m ^ bit] + packed[i].astype(F32)
                    del held[m]
        for held in halves:
            pieces.append(held[0])
            squares = squares + jnp.sum(held[0] * held[0])

    total = jnp.broadcast_to(squares, (8, 128))
    total = total + flip(total, "fsdp", n_fsdp, 1)
    total = total + sum(flip(total, "fsdp", n_fsdp, m) for m in keeps[1:])
    total = total + sum(
        lax.ppermute(total, "tp", [(i, (i + k) % n_tp) for i in range(n_tp)]) for k in range(1, n_tp)
    )
    return scaled(total, pieces, total_d * total_p)


def solution(mesh):
    n_fsdp, n_tp = mesh.shape["fsdp"], mesh.shape["tp"]
    placed = (P("fsdp", None), P("fsdp", None), P("fsdp"), P("fsdp", "tp"), P("fsdp", "tp"))

    def body(*args):
        return per_device(n_fsdp, n_tp, *args)

    return jax.shard_map(
        body, mesh=mesh, in_specs=placed, out_specs=P("fsdp", "tp"), check_vma=False
    )
```

```python
import functools

import jax
import jax.numpy as jnp
from jax import lax
from jax.experimental import pallas as pl
from jax.experimental.pallas import tpu as pltpu
from jax.sharding import PartitionSpec as P


LEN = 256
BF = jnp.bfloat16
F32 = jnp.float32


def dot(left, right, dims):
    return lax.dot_general(left, right, ((dims[:1], dims[1:]), ((), ())), preferred_element_type=F32)


def flip(value, axis, size, bit):
    return lax.ppermute(value, axis, [(i, i ^ bit) for i in range(size)])


def after(value, *others):
    return lax.optimization_barrier((value,) + others)[0]


def masks_of(bits):
    masks = [0]
    for bit in bits:
        masks = masks + [m | bit for m in masks]
    return sorted(masks, key=lambda m: (bin(m).count("1"), m))


def gather_near(shard, size, bits):
    return {0: shard, **{bit: flip(shard, "fsdp", size, bit) for bit in bits}}


def gather_far(got, size, bits, gate):
    got = {m: after(block, gate) for m, block in got.items()}
    half = got[0].shape[0] // 2
    low = high = None
    for mask in masks_of(bits)[1 + len(bits) :]:
        inside = [bit for bit in bits if mask & bit]
        first, last = inside[0], inside[-1]
        low, high = got[mask ^ last][:half], got[mask ^ first][half:]
        low, high = flip(low, "fsdp", size, last), flip(high, "fsdp", size, first)
        got[mask] = jnp.concatenate([low, high], axis=0)
    for mask in masks_of(bits):
        got[mask ^ 1] = flip(got[mask], "fsdp", size, 1)
    return got, (low, high)


def order_kernel(places, lengths, act_ref, cot_ref, out_ref):
    tokens = act_ref.shape[0]
    out_ref[:tokens, :] = act_ref[...]
    position = lax.broadcasted_iota(jnp.int32, (LEN, act_ref.shape[1]), 0)
    for i in range(tokens // LEN):
        rows = cot_ref[i * LEN : (i + 1) * LEN, :]
        kept = jnp.where(position < lengths[i], rows, jnp.zeros_like(rows))
        out_ref[tokens + i * LEN : tokens + (i + 1) * LEN, :] = kept


def ordered(places, lengths, activations, cotangent, cols):
    tokens, total = activations.shape
    if cols % 128:
        keep = (jnp.arange(LEN, dtype=jnp.int32)[None, :] < lengths[:, None]).reshape(-1)
        kept = jnp.where(keep[:, None], cotangent, jnp.zeros_like(cotangent))
        both = jnp.concatenate([activations, kept], axis=0)
        return jnp.concatenate(
            [lax.dynamic_slice_in_dim(both, p * cols, cols, axis=1) for p in places], axis=1
        )
    block = pl.BlockSpec((tokens, cols), lambda m, where, _: (0, where[m]))
    return pl.pallas_call(
        order_kernel,
        out_shape=jax.ShapeDtypeStruct((2 * tokens, total), activations.dtype),
        grid_spec=pltpu.PrefetchScalarGridSpec(
            num_scalar_prefetch=2,
            grid=(total // cols,),
            in_specs=[block, block],
            out_specs=pl.BlockSpec((2 * tokens, cols), lambda m, where, _: (0, m)),
        ),
        compiler_params=pltpu.CompilerParams(vmem_limit_bytes=24 << 20),
        cost_estimate=pl.CostEstimate(flops=0, bytes_accessed=8 * tokens * total, transcendentals=0),
    )(jnp.stack(places), lengths, activations, cotangent)


def scale_kernel(count, total_ref, *refs):
    refs, out_ref = refs[:-1], refs[-1]
    cols = refs[0].shape[1]
    scale = lax.rsqrt(total_ref[0:1, :] / count + 1e-06)
    scale = jnp.concatenate([scale] * (cols // 128), axis=1)
    for i, ref in enumerate(refs):
        out_ref[:, i * cols : (i + 1) * cols] = (ref[...] * scale).astype(out_ref.dtype)


def scaled(total, pieces, count):
    rows, cols = pieces[0].shape
    if cols % 128:
        scale = lax.rsqrt(total[0, 0] / count + 1e-06)
        return jnp.concatenate([(piece * scale).astype(BF) for piece in pieces], axis=1)
    return pl.pallas_call(
        functools.partial(scale_kernel, count),
        out_shape=jax.ShapeDtypeStruct((rows, cols * len(pieces)), BF),
        compiler_params=pltpu.CompilerParams(vmem_limit_bytes=16 << 20),
    )(total, *pieces)


def per_device(n_fsdp, n_tp, activations, cotangent, lengths, grow_operator, proxy_weight):
    me = lax.axis_index("fsdp")
    at = lax.axis_index("tp")
    bits = []
    while 2 << len(bits) < n_fsdp:
        bits.append(2 << len(bits))
    keeps = masks_of(bits)
    order = keeps + [m ^ 1 for m in keeps]
    tokens = activations.shape[0]
    rows, width = grow_operator.shape
    depth = proxy_weight.shape[0]
    split = len(keeps) * rows
    total_d, total_p = rows * n_fsdp, width * n_tp
    chunks = width // depth
    close = n_fsdp - 2
    last = n_tp - 1

    both = ordered([me ^ m for m in order], lengths, activations, cotangent, rows)

    w = gather_near(grow_operator, n_fsdp, bits)
    w, ends = gather_far(w, n_fsdp, bits, both)
    r = gather_near(after(proxy_weight, *ends), n_fsdp, bits)

    acc = dot(both, jnp.concatenate([w[m] for m in order], axis=0), (1, 0))
    forward = acc[:tokens].astype(BF)
    back = acc[tokens:].astype(BF)

    r, _ = gather_far(r, n_fsdp, bits, forward)

    assert chunks == 2
    odd = me % 2
    r_all = jnp.zeros((total_p, width), BF)
    for m in range(close):
        r_all = lax.dynamic_update_slice_in_dim(r_all, r[m], (m ^ odd) * depth, axis=0)
    product_near = dot(forward, r_all[: close * depth], (1, 1)).astype(BF)
    for m in range(close, n_fsdp):
        block = after(r[m], product_near)
        r_all = lax.dynamic_update_slice_in_dim(r_all, block, (m ^ odd) * depth, axis=0)
    product_far = [dot(forward, r[close + i], (1, 1)).astype(BF) for i in range(2)]

    def place(c, owner):
        return me ^ (jnp.clip(owner, 0, last) * chunks + c)

    def trade(value, pairs, parity):
        pairs = [pair for pair in pairs if min(pair) % 2 == parity]
        return lax.ppermute(value, "tp", pairs) if pairs else None

    def add(*terms):
        terms = [term for term in terms if term is not None]
        return functools.reduce(lambda one, two: one + two, terms) if terms else None

    evens, odds = [back], [back]
    for hop in range(last):
        pairs = [(i, i + 1) for i in range(hop, last)]
        pairs += [(last - one, last - two) for one, two in pairs]
        even = trade(odds[-1], pairs, 0)
        odd_ = trade(evens[-1], pairs, 1)
        evens.append(even)
        odds.append(odd_)

    delta = None
    for hop in sorted(range(n_tp), key=lambda hop: max(hop, n_tp - hop) if hop else 0):
        piece = back
        if hop:
            below, above = add(evens[hop], odds[n_tp - hop]), add(odds[hop], evens[n_tp - hop])
            piece = jnp.where(at % 2 == 1, below, above)
        owner = lax.rem(at - hop + n_tp, n_tp)
        block = lax.dynamic_slice_in_dim(r_all, (me // 2 ^ owner) * width, width, axis=0)
        part = dot(piece, block, (1, 0))
        delta = part if delta is None else delta + part
    delta = delta.astype(BF)

    def partial(products, c, owner):
        block = place(c, owner)
        start = (jnp.minimum(block, close - 1) ^ odd) * depth
        near = lax.dynamic_slice_in_dim(products[0], start, depth, axis=1)
        far = jnp.where(block == close, *products[1:])
        return jnp.where(block < close, near, far).astype(F32)

    products = (product_near, *product_far)
    sums, own = [], []
    for c in range(chunks):
        if c:
            products = lax.optimization_barrier(products + (sums[-1][0][0],))[:3]
        even = odd_ = None
        hops = []
        for hop in range(1, n_tp):
            pairs = [(i, i + 1) for i in range(hop)]
            pairs += [(last - one, last - two) for one, two in pairs]
            ends = (at + n_tp - hop, at + hop - n_tp)
            up_even = at % 2 == 0
            to_even = add(partial(products, c, jnp.where(up_even, *ends)), odd_).astype(BF)
            to_odd = add(partial(products, c, jnp.where(up_even, *ends[::-1])), even).astype(BF)
            to_even, to_odd = lax.optimization_barrier((to_even, to_odd))
            even = trade(to_even, pairs, 0)
            odd_ = trade(to_odd, pairs, 1)
            hops.append([x for x in (even, odd_) if x is not None])
        sums.append(hops)
        own.append(partial(products, c, at).astype(BF))

    squares = jnp.zeros((), F32)
    pieces = []
    for c in range(chunks):
        parts = sums[c][-1]
        if c + 1 < chunks:
            parts = [after(part, *sums[c + 1][-2]) for part in parts]
        proxy_out = add(own[c].astype(F32), *[part.astype(F32) for part in parts]).astype(BF)
        values = jnp.concatenate([delta[:, c * depth : (c + 1) * depth], proxy_out], axis=0)

        send = dot(both[:, split:], values, (0, 0)).astype(BF)
        arrived = flip(send, "fsdp", n_fsdp, 1)
        keep = after(dot(both[:, :split], values, (0, 0)).astype(BF), values)
        pair = (keep.astype(F32) + arrived.astype(F32)).astype(BF)
        blocks = {m: pair[i * rows : (i + 1) * rows] for i, m in enumerate(keeps)}
        half = depth // 2
        halves = [
            {m: blocks[m][:, n * half : (n + 1) * half].astype(F32) for m in keeps} for n in range(2)
        ]
        for turn in range(len(bits)):
            arrived = []
            for held, bit in zip(halves, (bits[turn], bits[-1 - turn])):
                packed = jnp.stack([held[m].astype(BF) for m in held if m & bit])
                arrived.append(flip(packed, "fsdp", n_fsdp, bit))
            arrived = lax.optimization_barrier(tuple(arrived))
            for held, bit, packed in zip(halves, (bits[turn], bits[-1 - turn]), arrived):
                for i, m in enumerate([m for m in held if m & bit]):
                    held[m ^ bit] = held[m ^ bit] + packed[i].astype(F32)
                    del held[m]
        for held in halves:
            pieces.append(held[0])
            squares = squares + jnp.sum(held[0] * held[0])

    total = jnp.broadcast_to(squares, (8, 128))
    total = total + flip(total, "fsdp", n_fsdp, 1)
    total = total + sum(flip(total, "fsdp", n_fsdp, m) for m in keeps[1:])
    total = total + sum(
        lax.ppermute(total, "tp", [(i, (i + k) % n_tp) for i in range(n_tp)]) for k in range(1, n_tp)
    )
    return scaled(total, pieces, total_d * total_p)


def solution(mesh):
    n_fsdp, n_tp = mesh.shape["fsdp"], mesh.shape["tp"]
    placed = (P("fsdp", None), P("fsdp", None), P("fsdp"), P("fsdp", "tp"), P("fsdp", "tp"))

    def body(*args):
        return per_device(n_fsdp, n_tp, *args)

    return jax.shard_map(
        body, mesh=mesh, in_specs=placed, out_specs=P("fsdp", "tp"), check_vma=False
    )
```

```python
import functools

import jax
import jax.numpy as jnp
from jax import lax
from jax.experimental import pallas as pl
from jax.experimental.pallas import tpu as pltpu
from jax.sharding import PartitionSpec as P


LEN = 256
BF = jnp.bfloat16
F32 = jnp.float32


def dot(left, right, dims):
    return lax.dot_general(left, right, ((dims[:1], dims[1:]), ((), ())), preferred_element_type=F32)


def flip(value, axis, size, bit):
    return lax.ppermute(value, axis, [(i, i ^ bit) for i in range(size)])


def after(value, *others):
    return lax.optimization_barrier((value,) + others)[0]


def masks_of(bits):
    masks = [0]
    for bit in bits:
        masks = masks + [m | bit for m in masks]
    return sorted(masks, key=lambda m: (bin(m).count("1"), m))


def gather_near(shard, size, bits):
    return {0: shard, **{bit: flip(shard, "fsdp", size, bit) for bit in bits}}


def gather_far(got, size, bits, gate):
    got = {m: after(block, gate) for m, block in got.items()}
    half = got[0].shape[0] // 2
    low = high = None
    for mask in masks_of(bits)[1 + len(bits) :]:
        inside = [bit for bit in bits if mask & bit]
        first, last = inside[0], inside[-1]
        low, high = got[mask ^ last][:half], got[mask ^ first][half:]
        low, high = flip(low, "fsdp", size, last), flip(high, "fsdp", size, first)
        got[mask] = jnp.concatenate([low, high], axis=0)
    for mask in masks_of(bits):
        got[mask ^ 1] = flip(got[mask], "fsdp", size, 1)
    return got, (low, high)


def order_kernel(places, lengths, act_ref, cot_ref, out_ref):
    tokens = act_ref.shape[0]
    out_ref[:tokens, :] = act_ref[...]
    position = lax.broadcasted_iota(jnp.int32, (LEN, act_ref.shape[1]), 0)
    for i in range(tokens // LEN):
        rows = cot_ref[i * LEN : (i + 1) * LEN, :]
        kept = jnp.where(position < lengths[i], rows, jnp.zeros_like(rows))
        out_ref[tokens + i * LEN : tokens + (i + 1) * LEN, :] = kept


def ordered(places, lengths, activations, cotangent, cols):
    tokens, total = activations.shape
    if cols % 128:
        keep = (jnp.arange(LEN, dtype=jnp.int32)[None, :] < lengths[:, None]).reshape(-1)
        kept = jnp.where(keep[:, None], cotangent, jnp.zeros_like(cotangent))
        both = jnp.concatenate([activations, kept], axis=0)
        return jnp.concatenate(
            [lax.dynamic_slice_in_dim(both, p * cols, cols, axis=1) for p in places], axis=1
        )
    block = pl.BlockSpec((tokens, cols), lambda m, where, _: (0, where[m]))
    return pl.pallas_call(
        order_kernel,
        out_shape=jax.ShapeDtypeStruct((2 * tokens, total), activations.dtype),
        grid_spec=pltpu.PrefetchScalarGridSpec(
            num_scalar_prefetch=2,
            grid=(total // cols,),
            in_specs=[block, block],
            out_specs=pl.BlockSpec((2 * tokens, cols), lambda m, where, _: (0, m)),
        ),
        compiler_params=pltpu.CompilerParams(vmem_limit_bytes=24 << 20),
        cost_estimate=pl.CostEstimate(flops=0, bytes_accessed=8 * tokens * total, transcendentals=0),
    )(jnp.stack(places), lengths, activations, cotangent)


def scale_kernel(count, total_ref, *refs):
    refs, out_ref = refs[:-1], refs[-1]
    cols = refs[0].shape[1]
    scale = lax.rsqrt(total_ref[0:1, :] / count + 1e-06)
    scale = jnp.concatenate([scale] * (cols // 128), axis=1)
    for i, ref in enumerate(refs):
        out_ref[:, i * cols : (i + 1) * cols] = (ref[...] * scale).astype(out_ref.dtype)


def scaled(total, pieces, count):
    rows, cols = pieces[0].shape
    if cols % 128:
        scale = lax.rsqrt(total[0, 0] / count + 1e-06)
        return jnp.concatenate([(piece * scale).astype(BF) for piece in pieces], axis=1)
    return pl.pallas_call(
        functools.partial(scale_kernel, count),
        out_shape=jax.ShapeDtypeStruct((rows, cols * len(pieces)), BF),
        compiler_params=pltpu.CompilerParams(vmem_limit_bytes=16 << 20),
    )(total, *pieces)


def unset(rows, cols):
    return pl.pallas_call(
        lambda out_ref: None,
        out_shape=jax.ShapeDtypeStruct((rows, cols), BF),
        out_specs=pl.BlockSpec(memory_space=pl.ANY),
        name="unset",
    )()


def per_device(n_fsdp, n_tp, activations, cotangent, lengths, grow_operator, proxy_weight):
    me = lax.axis_index("fsdp")
    at = lax.axis_index("tp")
    bits = []
    while 2 << len(bits) < n_fsdp:
        bits.append(2 << len(bits))
    keeps = masks_of(bits)
    order = keeps + [m ^ 1 for m in keeps]
    tokens = activations.shape[0]
    rows, width = grow_operator.shape
    depth = proxy_weight.shape[0]
    split = len(keeps) * rows
    total_d, total_p = rows * n_fsdp, width * n_tp
    chunks = width // depth
    close = n_fsdp - 2
    last = n_tp - 1

    both = ordered([me ^ m for m in order], lengths, activations, cotangent, rows)

    w = gather_near(grow_operator, n_fsdp, bits)
    w, ends = gather_far(w, n_fsdp, bits, both)
    r = gather_near(after(proxy_weight, *ends), n_fsdp, bits)

    acc = dot(both, jnp.concatenate([w[m] for m in order], axis=0), (1, 0))
    forward = acc[:tokens].astype(BF)
    back = acc[tokens:].astype(BF)

    r, _ = gather_far(r, n_fsdp, bits, forward)

    assert chunks == 2
    odd = me % 2
    r_near = jnp.concatenate([r[m] for m in range(close)], axis=0)
    product_near = dot(forward, r_near, (1, 1)).astype(BF)
    product_far = [dot(forward, r[close + i], (1, 1)).astype(BF) for i in range(2)]
    r_all = unset(total_p, width)
    for m in range(n_fsdp):
        block = after(r[m], product_far[0])
        r_all = lax.dynamic_update_slice_in_dim(r_all, block, (m ^ odd) * depth, axis=0)

    def place(c, owner):
        return me ^ (jnp.clip(owner, 0, last) * chunks + c)

    def trade(value, pairs, parity):
        pairs = [pair for pair in pairs if min(pair) % 2 == parity]
        return lax.ppermute(value, "tp", pairs) if pairs else None

    def add(*terms):
        terms = [term for term in terms if term is not None]
        return functools.reduce(lambda one, two: one + two, terms) if terms else None

    evens, odds = [back], [back]
    for hop in range(last):
        pairs = [(i, i + 1) for i in range(hop, last)]
        pairs += [(last - one, last - two) for one, two in pairs]
        even = trade(odds[-1], pairs, 0)
        odd_ = trade(evens[-1], pairs, 1)
        evens.append(even)
        odds.append(odd_)

    delta = None
    for hop in sorted(range(n_tp), key=lambda hop: max(hop, n_tp - hop) if hop else 0):
        piece = back
        if hop:
            below, above = add(evens[hop], odds[n_tp - hop]), add(odds[hop], evens[n_tp - hop])
            piece = jnp.where(at % 2 == 1, below, above)
        owner = lax.rem(at - hop + n_tp, n_tp)
        block = lax.dynamic_slice_in_dim(r_all, (me // 2 ^ owner) * width, width, axis=0)
        part = dot(piece, block, (1, 0))
        delta = part if delta is None else delta + part
    delta = delta.astype(BF)

    def partial(products, c, owner):
        block = place(c, owner)
        start = jnp.minimum(block, close - 1) * depth
        near = lax.dynamic_slice_in_dim(products[0], start, depth, axis=1)
        far = jnp.where(block == close, *products[1:])
        return jnp.where(block < close, near, far).astype(F32)

    products = (product_near, *product_far)
    sums, own = [], []
    for c in range(chunks):
        if c:
            products = lax.optimization_barrier(products + (sums[-1][0][0],))[:3]
        even = odd_ = None
        hops = []
        for hop in range(1, n_tp):
            pairs = [(i, i + 1) for i in range(hop)]
            pairs += [(last - one, last - two) for one, two in pairs]
            ends = (at + n_tp - hop, at + hop - n_tp)
            up_even = at % 2 == 0
            to_even = add(partial(products, c, jnp.where(up_even, *ends)), odd_).astype(BF)
            to_odd = add(partial(products, c, jnp.where(up_even, *ends[::-1])), even).astype(BF)
            to_even, to_odd = lax.optimization_barrier((to_even, to_odd))
            even = trade(to_even, pairs, 0)
            odd_ = trade(to_odd, pairs, 1)
            hops.append([x for x in (even, odd_) if x is not None])
        sums.append(hops)
        own.append(partial(products, c, at).astype(BF))

    squares = jnp.zeros((), F32)
    pieces = []
    for c in range(chunks):
        parts = sums[c][-1]
        if c + 1 < chunks:
            parts = [after(part, *sums[c + 1][-2]) for part in parts]
        proxy_out = add(own[c].astype(F32), *[part.astype(F32) for part in parts]).astype(BF)
        values = jnp.concatenate([delta[:, c * depth : (c + 1) * depth], proxy_out], axis=0)

        send = dot(both[:, split:], values, (0, 0)).astype(BF)
        arrived = flip(send, "fsdp", n_fsdp, 1)
        keep = after(dot(both[:, :split], values, (0, 0)).astype(BF), values)
        pair = (keep.astype(F32) + arrived.astype(F32)).astype(BF)
        blocks = {m: pair[i * rows : (i + 1) * rows] for i, m in enumerate(keeps)}
        half = depth // 2
        halves = [
            {m: blocks[m][:, n * half : (n + 1) * half].astype(F32) for m in keeps} for n in range(2)
        ]
        for turn in range(len(bits)):
            arrived = []
            for held, bit in zip(halves, (bits[turn], bits[-1 - turn])):
                packed = jnp.stack([held[m].astype(BF) for m in held if m & bit])
                arrived.append(flip(packed, "fsdp", n_fsdp, bit))
            arrived = lax.optimization_barrier(tuple(arrived))
            for held, bit, packed in zip(halves, (bits[turn], bits[-1 - turn]), arrived):
                for i, m in enumerate([m for m in held if m & bit]):
                    held[m ^ bit] = held[m ^ bit] + packed[i].astype(F32)
                    del held[m]
        for held in halves:
            pieces.append(held[0])
            squares = squares + jnp.sum(held[0] * held[0])

    total = jnp.broadcast_to(squares, (8, 128))
    total = total + flip(total, "fsdp", n_fsdp, 1)
    total = total + sum(flip(total, "fsdp", n_fsdp, m) for m in keeps[1:])
    total = total + sum(flip(total, "tp", n_tp, k) for k in range(1, n_tp))
    return scaled(total, pieces, total_d * total_p)


def solution(mesh):
    n_fsdp, n_tp = mesh.shape["fsdp"], mesh.shape["tp"]
    placed = (P("fsdp", None), P("fsdp", None), P("fsdp"), P("fsdp", "tp"), P("fsdp", "tp"))

    def body(*args):
        return per_device(n_fsdp, n_tp, *args)

    return jax.shard_map(
        body, mesh=mesh, in_specs=placed, out_specs=P("fsdp", "tp"), check_vma=False
    )
```
